32 devices in a mesh: gx: 4 (over y, x), gy: 4 (over z), gz: 2 (over core).
Axes of the slice: x: 2, y: 2, z: 4, core: 2. Of those that a mesh axis runs over, the one named last changes fastest.
Arguments:
- populations: float32 [19, 32, 32, 512], P(None, 'gx', 'gz', 'gy'), may hold values from 0.005 to 0.6, as said below
- link_cell: int32 [4, 2, 4, 1024], P('gx', 'gz', 'gy'), may hold values from 0 to 16383, as said below
- link_dir: int32 [4, 2, 4, 1024], P('gx', 'gz', 'gy'), may hold values from 0 to 18, as said below
- link_slot: int32 [4, 2, 4, 1024], P('gx', 'gz', 'gy'), may hold values from 0 to 127, as said below
- link_arm: float32 [3, 4, 2, 4, 1024], P(None, 'gx', 'gz', 'gy'), may hold values from -6 to 6
- brick_bodies: int32 [4, 2, 4, 128], P('gx', 'gz', 'gy'), may hold values from 0 to 2047, as said below
- body_pos: float32 [3, 2048], P(None, ('gx', 'gy')), may hold values from -1 to 1
- body_quat: float32 [4, 2048], P(None, ('gx', 'gy')), may hold values from -1 to 1, as said below
- body_vel: float32 [3, 2048], P(None, ('gx', 'gy')), may hold values from -0.4 to 0.4
- body_spin: float32 [3, 2048], P(None, ('gx', 'gy')), may hold values from -0.4 to 0.4
- inv_mass: float32 [2048], P(('gx', 'gy')), may hold values from 0.5 to 4
- inv_inertia: float32 [3, 2048], P(None, ('gx', 'gy')), may hold values from 0.2 to 2
Outputs:
- next_populations: float32 [19, 32, 32, 512], P(None, 'gx', 'gz', 'gy')
- body_next: float32 [13, 2048], P(None, ('gx', 'gy'))
The draws below stay inside these ranges and needn't reach their ends.
Inputs may be any that keep to these rules, and one draw needn't show every extreme that they name: `populations`: every entry is positive, and the density (sum over the 19 directions) at every cell lies between 0.5 and 1.6. `link_cell`: within a brick all entries name different cells. `link_dir`: within a brick the used entries (direction 1 to 18) come first, unused ones have direction 0; some brick uses all 1024 entries in every draw. `link_slot`: unused entries hold 0. `brick_bodies`: each brick lists 128 different bodies; owner k holds bodies k*128 to (k+1)*128 - 1; a brick lists at most 16 bodies of one owner, and exactly 16 of some owner in every brick. `body_quat`: unit quaternions.
All inputs are finite; a program needn't handle non-finite values.
Results may differ from the reference program's by a relative error of at most 0.00013.
Values sent between devices are 32-bit elements; how exact they have to be, the bound alone decides.
A program may use at most 64 MiB of HBM per device.

```python
import math
import jax
import jax.numpy as jnp
import numpy as np
from jax import lax

CX = 8
CZ = 16
CY = 128
SLOTS = 128
BODY_OWN = 128
LINKS = 1024
NB = 2048
CAP = 16
NX = 32
NZ = 32
NY = 512
N_GX = 4
N_GY = 4
N_GZ = 2


lattice_vel = np.array([[0, 0, 0], [1, 0, 0], [-1, 0, 0], [0, 1, 0], [0, -1, 0], [0, 0, 1], [0, 0, -1], [1, 1, 0], [-1, -1, 0], [1, -1, 0], [-1, 1, 0], [1, 0, 1], [-1, 0, -1], [1, 0, -1], [-1, 0, 1], [0, 1, 1], [0, -1, -1], [0, 1, -1], [0, -1, 1]])


lattice_wt = np.array([1.0 / 3.0] + [1.0 / 18.0] * 6 + [1.0 / 36.0] * 12)


def draw_populations(key, part):
    key_dens, key_flow, key_noise = jax.random.split(jax.random.fold_in(key, 3), 3)
    shape = (NX, NZ, NY)
    density = jax.random.uniform(key_dens, shape, jnp.float32, 0.9, 1.1)
    flows = jnp.clip(0.05 * jax.random.normal(key_flow, (3,) + shape, jnp.float32), -0.15, 0.15)
    noise = jnp.clip(0.1 * jax.random.normal(key_noise, (19,) + shape, jnp.float32), -0.3, 0.3)
    speed_sq = flows[0] * flows[0] + flows[1] * flows[1] + flows[2] * flows[2]
    result = []
    for direction in range(19):
        proj = float(lattice_vel[direction, 0]) * flows[0] + float(lattice_vel[direction, 1]) * flows[1] + float(lattice_vel[direction, 2]) * flows[2]
        equil = float(lattice_wt[direction]) * density * (1.0 + 3.0 * proj + 4.5 * proj * proj - 1.5 * speed_sq)
        result.append(equil * (1.0 + noise[direction]))
    return jnp.stack(result).astype(jnp.float32)


def link_fields(key):
    base = jax.random.fold_in(key, 7)
    key_cell, key_perm, key_dir, key_slot, key_count = jax.random.split(base, 5)
    bricks = N_GX * N_GZ * N_GY
    cells = CX * CZ * CY
    stride = cells // LINKS
    entry = jnp.arange(LINKS, dtype=jnp.int32)
    offsets = jax.random.randint(key_cell, (bricks, LINKS), 0, stride, dtype=jnp.int32)
    cell_idx = entry[None, :] * stride + offsets
    scores = jax.random.randint(key_perm, (bricks, LINKS), 0, 2 ** 18, dtype=jnp.int32) * LINKS + entry[None, :]
    order = jnp.argsort(scores, axis=1)
    cell_idx = jnp.take_along_axis(cell_idx, order, axis=1)
    layer_z = jnp.arange(bricks, dtype=jnp.int32) // N_GY % N_GZ
    counts = jax.random.randint(key_count, (bricks,), LINKS // 4, LINKS // 2 + 1, dtype=jnp.int32)
    counts = jnp.where(layer_z == 0, LINKS, counts)
    live = entry[None, :] < counts[:, None]
    dirs = jnp.where(live, jax.random.randint(key_dir, (bricks, LINKS), 1, 19, dtype=jnp.int32), 0)
    slots = jnp.where(live, jax.random.randint(key_slot, (bricks, LINKS), 0, SLOTS, dtype=jnp.int32), 0)
    shape = (N_GX, N_GZ, N_GY, LINKS)
    return (cell_idx.reshape(shape), dirs.reshape(shape), slots.reshape(shape))


def draw_link_cell(key, part):
    return link_fields(key)[0]


def draw_link_dir(key, part):
    return link_fields(key)[1]


def draw_link_slot(key, part):
    return link_fields(key)[2]


def draw_brick_bodies(key, part):
    key_perm, key_pick, key_offs = jax.random.split(jax.random.fold_in(key, 11), 3)
    bricks = N_GX * N_GZ * N_GY
    owners = N_GX * N_GY
    total = owners * CAP
    entry = jnp.arange(total, dtype=jnp.int32)
    scores = jax.random.randint(key_perm, (bricks, total), 0, 2 ** 18, dtype=jnp.int32) * total + entry[None, :]
    chosen = jax.random.randint(key_pick, (bricks,), 0, owners, dtype=jnp.int32)
    scores = jnp.where((entry // CAP)[None, :] == chosen[:, None], -total + (entry % CAP)[None, :], scores)
    order = jnp.argsort(scores, axis=1)[:, :SLOTS]
    owner_of = order // CAP
    copy_of = order % CAP
    offsets = jax.random.randint(key_offs, (bricks, owners), 0, BODY_OWN, dtype=jnp.int32)
    base_off = jnp.take_along_axis(offsets, owner_of, axis=1)
    local = (base_off + copy_of * (BODY_OWN // CAP)) % BODY_OWN
    return (owner_of * BODY_OWN + local).reshape(N_GX, N_GZ, N_GY, SLOTS)


def draw_body_quat(key, part):
    base = jax.random.fold_in(key, 13)
    raw = jax.random.normal(base, (4, NB), jnp.float32)
    return (raw / jnp.sqrt(jnp.sum(raw * raw, 0, keepdims=True) + 1e-12)).astype(jnp.float32)


def shard_levels(key, dims, pieces, low, largest):
    def one(dim, parts):
        steps = jax.random.uniform(jax.random.fold_in(jax.random.fold_in(key, 6), dim), (parts,), jnp.float32, low / len(pieces), largest / len(pieces))
        return jnp.repeat(jnp.exp(steps), dims[dim] // parts).reshape((-1,) + (1,) * (len(dims) - dim - 1))

    factor_of = one(*pieces[0])
    for cut in pieces[1:]:
        factor_of = factor_of * one(*cut)
    return factor_of


def centred(rng, dims, scale, reach, cuts=(), kind=jnp.bfloat16):
    values = jax.random.normal(rng, dims, jnp.float32) * scale
    if len(cuts) > 0:
        values = shard_levels(rng, dims, cuts, -0.22, 0.18) * values
    return jnp.clip(values, min=-reach, max=reach).astype(kind)


def setup_inputs(seed: int = 0) -> dict:
    arg_keys = jax.random.split(jax.random.key(seed), 13)
    populations = draw_populations(jax.random.fold_in(arg_keys[12], 71), 0)
    link_cell = draw_link_cell(jax.random.fold_in(arg_keys[12], 71), 0)
    link_dir = draw_link_dir(jax.random.fold_in(arg_keys[12], 71), 0)
    link_slot = draw_link_slot(jax.random.fold_in(arg_keys[12], 71), 0)
    link_arm = centred(arg_keys[4], (3, N_GX, N_GZ, N_GY, LINKS), 2.0, 6.0, ((1, 4), (2, 2), (3, 4)), jnp.float32)
    brick_bodies = draw_brick_bodies(jax.random.fold_in(arg_keys[12], 71), 0)
    body_pos = jnp.clip(jax.random.uniform(arg_keys[6], (3, NB), jnp.float32, -1.0, 1.0) * shard_levels(arg_keys[6], (3, NB), ((1, 16),), -0.4, 0.0), -1.0, 1.0)
    body_quat = draw_body_quat(jax.random.fold_in(arg_keys[12], 71), 0)
    body_vel = centred(arg_keys[8], (3, NB), 0.1, 0.4, ((1, 16),), jnp.float32)
    body_spin = centred(arg_keys[9], (3, NB), 0.1, 0.4, ((1, 16),), jnp.float32)
    inv_mass = jnp.clip(jnp.exp(math.log(4.0) - 2.0794415 * jax.random.uniform(arg_keys[10], (NB,), jnp.float32) ** shard_levels(arg_keys[10], (NB,), ((0, 16),), -0.2, 0.2)), 0.5, 4.0)
    inv_inertia = jnp.clip(jnp.exp(math.log(2.0) - 2.3025851 * jax.random.uniform(arg_keys[11], (3, NB), jnp.float32) ** shard_levels(arg_keys[11], (3, NB), ((1, 16),), -0.2, 0.2)), 0.2, 2.0)
    return dict(populations=populations, link_cell=link_cell, link_dir=link_dir, link_slot=link_slot, link_arm=link_arm, brick_bodies=brick_bodies, body_pos=body_pos, body_quat=body_quat, body_vel=body_vel, body_spin=body_spin, inv_mass=inv_mass, inv_inertia=inv_inertia)


lattice_vel = np.array([[0, 0, 0], [1, 0, 0], [-1, 0, 0], [0, 1, 0], [0, -1, 0], [0, 0, 1], [0, 0, -1], [1, 1, 0], [-1, -1, 0], [1, -1, 0], [-1, 1, 0], [1, 0, 1], [-1, 0, -1], [1, 0, -1], [-1, 0, 1], [0, 1, 1], [0, -1, -1], [0, 1, -1], [0, -1, 1]])
lattice_wt = np.array([1.0 / 3.0] + [1.0 / 18.0] * 6 + [1.0 / 36.0] * 12)
opposite_dir = np.array([0, 2, 1, 4, 3, 6, 5, 8, 7, 10, 9, 12, 11, 14, 13, 16, 15, 18, 17])
omega_relax = 1.25
grav_accel = 0.02

def collide(populations):
    density = populations[0]
    for direction in range(1, 19):
        density = density + populations[direction]
    flows = []
    for comp_index in range(3):
        total = jnp.zeros_like(density)
        for direction in range(19):
            if lattice_vel[direction, comp_index] == 1:
                total = total + populations[direction]
            elif lattice_vel[direction, comp_index] == -1:
                total = total - populations[direction]
        flows.append(total / density)
    speed_sq = flows[0] * flows[0] + flows[1] * flows[1] + flows[2] * flows[2]
    relaxed = []
    for direction in range(19):
        proj = float(lattice_vel[direction, 0]) * flows[0] + float(lattice_vel[direction, 1]) * flows[1] + float(lattice_vel[direction, 2]) * flows[2]
        equil = float(lattice_wt[direction]) * density * (1.0 + 3.0 * proj + 4.5 * proj * proj - 1.5 * speed_sq)
        relaxed.append(populations[direction] - omega_relax * (populations[direction] - equil))
    return jnp.stack(relaxed)

def link_terms(post_out, link_dirs, arm, motion_at):
    iota_dir = jnp.arange(19, dtype=jnp.int32)
    onehot = (link_dirs[None, :] == iota_dir[:, None]).astype(jnp.float32)
    table = jnp.asarray(np.concatenate([lattice_vel.T, lattice_wt[None, :]], 0), jnp.float32)
    coeffs = jnp.dot(table, onehot, precision=lax.Precision.HIGHEST)
    vel_x, vel_y, vel_z = (coeffs[0], coeffs[1], coeffs[2])
    weight = coeffs[3]
    opp_table = jnp.asarray(opposite_dir, jnp.int32)
    opp_dir = lax.optimization_barrier(jnp.sum(opp_table[:, None] * (link_dirs[None, :] == iota_dir[:, None]).astype(jnp.int32), 0))
    wall_x = motion_at[0] + motion_at[4] * arm[2] - motion_at[5] * arm[1]
    wall_y = motion_at[1] + motion_at[5] * arm[0] - motion_at[3] * arm[2]
    wall_z = motion_at[2] + motion_at[3] * arm[1] - motion_at[4] * arm[0]
    proj = vel_x * wall_x + vel_y * wall_y + vel_z * wall_z
    bounce = post_out - 6.0 * weight * proj
    live = (link_dirs > 0).astype(jnp.float32)
    exchanged = (post_out + bounce) * live
    force_x, force_y, force_z = (vel_x * exchanged, vel_y * exchanged, vel_z * exchanged)
    torque_x = arm[1] * force_z - arm[2] * force_y
    torque_y = arm[2] * force_x - arm[0] * force_z
    torque_z = arm[0] * force_y - arm[1] * force_x
    loads = jnp.stack([force_x, force_y, force_z, torque_x, torque_y, torque_z])
    return (bounce, live, opp_dir, loads)

def integrate(body_pos, body_quat, body_vel, body_spin, inv_mass, inv_inertia, load):
    gravity = jnp.asarray(np.array([0.0, 0.0, -grav_accel]), jnp.float32)[:, None]
    velocity = body_vel + inv_mass[None, :] * load[0:3] + gravity
    quat_w, quat_x, quat_y, quat_z = (body_quat[0], body_quat[1], body_quat[2], body_quat[3])
    rotation = [[1.0 - 2.0 * (quat_y * quat_y + quat_z * quat_z), 2.0 * (quat_x * quat_y - quat_w * quat_z), 2.0 * (quat_x * quat_z + quat_w * quat_y)], [2.0 * (quat_x * quat_y + quat_w * quat_z), 1.0 - 2.0 * (quat_x * quat_x + quat_z * quat_z), 2.0 * (quat_y * quat_z - quat_w * quat_x)], [2.0 * (quat_x * quat_z - quat_w * quat_y), 2.0 * (quat_y * quat_z + quat_w * quat_x), 1.0 - 2.0 * (quat_x * quat_x + quat_y * quat_y)]]
    torque = load[3:6]
    frame_torque = [rotation[0][col] * torque[0] + rotation[1][col] * torque[1] + rotation[2][col] * torque[2] for col in range(3)]
    frame_accel = [inv_inertia[col] * frame_torque[col] for col in range(3)]
    accel = [rotation[row][0] * frame_accel[0] + rotation[row][1] * frame_accel[1] + rotation[row][2] * frame_accel[2] for row in range(3)]
    spin = body_spin + jnp.stack(accel)
    position = body_pos + velocity
    spin_x, spin_y, spin_z = (spin[0], spin[1], spin[2])
    delta_w = -(spin_x * quat_x + spin_y * quat_y + spin_z * quat_z)
    delta_x = spin_x * quat_w + spin_y * quat_z - spin_z * quat_y
    delta_y = spin_y * quat_w + spin_z * quat_x - spin_x * quat_z
    delta_z = spin_z * quat_w + spin_x * quat_y - spin_y * quat_x
    scale = lax.rsqrt(1.0 + 0.25 * (spin_x * spin_x + spin_y * spin_y + spin_z * spin_z))
    quat = jnp.stack([quat_w + 0.5 * delta_w, quat_x + 0.5 * delta_x, quat_y + 0.5 * delta_y, quat_z + 0.5 * delta_z]) * scale[None, :]
    return jnp.concatenate([position, quat, velocity, spin], 0)

def reference(populations, link_cell, link_dir, link_slot, link_arm, brick_bodies, body_pos, body_quat, body_vel, body_spin, inv_mass, inv_inertia):
    relaxed = collide(populations)
    read = jnp.stack([jnp.roll(relaxed[direction], (int(lattice_vel[direction, 0]), int(lattice_vel[direction, 2]), int(lattice_vel[direction, 1])), axis=(0, 1, 2)) for direction in range(19)])
    brick_x = jnp.arange(N_GX, dtype=jnp.int32)[:, None, None, None]
    brick_z = jnp.arange(N_GZ, dtype=jnp.int32)[None, :, None, None]
    brick_y = jnp.arange(N_GY, dtype=jnp.int32)[None, None, :, None]
    glob_x = (brick_x * CX + link_cell // (CZ * CY)).reshape(-1)
    glob_z = (brick_z * CZ + link_cell // CY % CZ).reshape(-1)
    glob_y = (brick_y * CY + link_cell % CY).reshape(-1)
    link_dirs = link_dir.reshape(-1)
    link_bodies = jnp.take_along_axis(brick_bodies, link_slot, axis=3).reshape(-1)
    arm = link_arm.reshape(3, -1)
    motion_at = jnp.concatenate([body_vel, body_spin], 0)[:, link_bodies]
    post_out = relaxed[link_dirs, glob_x, glob_z, glob_y]
    bounce, live, opp_dir, loads = link_terms(post_out, link_dirs, arm, motion_at)
    current = read[opp_dir, glob_x, glob_z, glob_y]
    next_populations = read.at[opp_dir, glob_x, glob_z, glob_y].add(live * (bounce - current))
    load = jax.ops.segment_sum(loads.T, link_bodies, num_segments=NB).T
    return (next_populations, integrate(body_pos, body_quat, body_vel, body_spin, inv_mass, inv_inertia, load))
```

```python
import functools

import jax
import jax.numpy as jnp
import numpy as np
from jax import lax
from jax.experimental import pallas as pl
from jax.experimental.pallas import tpu as pltpu
from jax.sharding import PartitionSpec as P

VEL = [
    (0, 0, 0), (1, 0, 0), (-1, 0, 0), (0, 1, 0), (0, -1, 0), (0, 0, 1), (0, 0, -1),
    (1, 1, 0), (-1, -1, 0), (1, -1, 0), (-1, 1, 0), (1, 0, 1), (-1, 0, -1), (1, 0, -1),
    (-1, 0, 1), (0, 1, 1), (0, -1, -1), (0, 1, -1), (0, -1, 1),
]
WT = [1.0 / 3.0] + [1.0 / 18.0] * 6 + [1.0 / 36.0] * 12
OPP = [0, 2, 1, 4, 3, 6, 5, 8, 7, 10, 9, 12, 11, 14, 13, 16, 15, 18, 17]
OMEGA = 1.25
POP_CHUNKS = 2
K1_VMEM = 48 * 1024 * 1024
K2_VMEM = 1024 * 1024
GRAV = 0.02
F32 = jnp.float32
BF16 = jnp.bfloat16


def dirs_of(comp, sign):
    return [d for d in range(19) if VEL[d][comp] == sign]


XD = (dirs_of(0, 1), dirs_of(0, -1))
YD = (dirs_of(1, 1), dirs_of(1, -1))
ZD = (dirs_of(2, 1), dirs_of(2, -1))
XZD = tuple([d for d in XD[s] if VEL[d][2] != 0] for s in range(2))


def split3(v):
    hi = v.astype(BF16).astype(F32)
    rest = v - hi
    mid = rest.astype(BF16).astype(F32)
    return hi, mid, rest - mid


def dot(a, b, ca, cb):
    return lax.dot_general(a, b, (((ca,), (cb,)), ((), ())), preferred_element_type=F32)


def stacked(v):
    return jnp.concatenate(split3(v), 0).astype(BF16)


def unstacked(v):
    k = v.shape[0] // 3
    return v[0:k] + v[k : 2 * k] + v[2 * k : 3 * k]


def kernel(
    sizes,
    pop_h, *rest,
):
    small_h, (nxt, bnext, pop), rest = rest[:11], rest[11:14], rest[14:]
    small, rest = rest[:11], rest[11:]
    step(sizes, pop_h, small_h, pop, *small, nxt, bnext, *rest)


def step(
    sizes, pop_h, small_h,
    pop, lcell, ldir, lslot, larm, bb_ref, bpos, bquat, bvel, bspin, imass, iinert,
    nxt, bnext,
    relaxed, sendx, xin, sendz, zin, sende, ein, sendy, yin, yflat, ycols,
    dmap, wmap, motion_own, motion_all, tiles, force_all, half, half_in,
    hs, hr, ms, mr, fs, fr, cs, cr, ps, ss,
):
    ngx, ngy = sizes
    owners = ngx * ngy
    span_x, span_z, span_y = pop.shape[1:]
    cells = span_x * span_z
    links = lcell.shape[-1]
    body_own = bvel.shape[1]
    slots = bb_ref.shape[-1]
    a, b, e = lax.axis_index("gx"), lax.axis_index("gy"), lax.axis_index("gz")
    me = a * ngy + b
    ap, am = lax.rem(a + 1, ngx), lax.rem(a + ngx - 1, ngx)
    bp, bm = lax.rem(b + 1, ngy), lax.rem(b + ngy - 1, ngy)
    oe = 1 - e

    def dev(x, y, z):
        return {"gx": x, "gy": y, "gz": z}

    def peer_of(offset):
        p = lax.rem(me + offset, owners)
        return p, dev(p // ngy, lax.rem(p, ngy), e)

    unroll = owners <= 16

    def loop(lo, hi, body):
        if unroll:
            for i in range(lo, hi):
                body(i)
        else:
            pl.loop(lo, hi)(body)

    small = (lcell, ldir, lslot, larm, bb_ref, bpos, bquat, bvel, bspin, imass, iinert)
    small_in = [
        pltpu.make_async_copy(src, dst, ss.at[k]) for k, (src, dst) in enumerate(zip(small_h, small))
    ]
    chunk = span_x // POP_CHUNKS
    pop_in = [
        pltpu.make_async_copy(
            pop_h.at[:, pl.ds(k * chunk, chunk)], pop.at[:, pl.ds(k * chunk, chunk)], ps.at[k]
        )
        for k in range(POP_CHUNKS)
    ]
    for k in (7, 8):
        small_in[k].start()
    for c in pop_in:
        c.start()
    for k in (0, 1, 2, 3, 4, 5, 6, 9, 10):
        small_in[k].start()

    barrier = pltpu.get_barrier_semaphore()

    def greet(o):
        pl.semaphore_signal(barrier, inc=1, device_id=peer_of(o)[1], device_id_type=pl.DeviceIdType.MESH)

    loop(1, owners, greet)
    others = [dev(a, b, oe), dev(ap, b, oe), dev(am, b, oe), dev(a, bp, oe), dev(a, bm, oe)]
    for t in others:
        pl.semaphore_signal(barrier, inc=1, device_id=t, device_id_type=pl.DeviceIdType.MESH)

    small_in[7].wait()
    small_in[8].wait()
    motion_own[...] = jnp.concatenate(
        [bvel[...], bspin[...], jnp.zeros((2, body_own), F32)], 0
    )
    motion_all[me] = motion_own[...]

    for x in range(span_x):
        if x % chunk == 0:
            pop_in[x // chunk].wait()
        for z in range(0, span_z, 8):
            f = [pop[d, x, z : z + 8, :] for d in range(19)]
            rho = f[0]
            for d in range(1, 19):
                rho = rho + f[d]
            inv = 1.0 / rho
            u = []
            for c in range(3):
                pos, neg = dirs_of(c, 1), dirs_of(c, -1)
                tot = f[pos[0]] - f[neg[0]]
                for p, q in zip(pos[1:], neg[1:]):
                    tot = tot + (f[p] - f[q])
                u.append(tot * inv)
            usq = 1.0 - 1.5 * (u[0] * u[0] + u[1] * u[1] + u[2] * u[2])
            rows = pl.ds(x * span_z + z, 8)
            keep = 1.0 - OMEGA
            relaxed[0, rows, :] = keep * f[0] + (OMEGA * WT[0]) * rho * usq
            for d in range(1, 19, 2):
                terms = [u[c] if VEL[d][c] > 0 else -u[c] for c in range(3) if VEL[d][c]]
                proj = terms[0] if len(terms) == 1 else terms[0] + terms[1]
                scale = (OMEGA * WT[d]) * rho
                even = scale * (usq + 4.5 * proj * proj)
                odd = scale * (3.0 * proj)
                relaxed[d, rows, :] = keep * f[d] + (even + odd)
                relaxed[d + 1, rows, :] = keep * f[d + 1] + (even - odd)

    for s in range(2):
        xe = (span_x - 1) if s == 0 else 0
        ze = (span_z - 1) if s == 0 else 0
        for j, d in enumerate(XD[s]):
            sendx[s, j] = relaxed[d, xe * span_z : (xe + 1) * span_z, :]
        for j, d in enumerate(ZD[s]):
            for x in range(span_x):
                r = x * span_z + ze
                sendz[s, j, x : x + 1, :] = relaxed[d, r : r + 1, :]
        sende[s] = jnp.zeros(sende.shape[1:], F32)
        for j, d in enumerate(XZD[s]):
            r = xe * span_z + ((span_z - 1) if VEL[d][2] > 0 else 0)
            sende[s, j : j + 1, :] = relaxed[d, r : r + 1, :]
    lane = lax.broadcasted_iota(jnp.int32, (cells, span_y), 1)
    pack = jnp.zeros((cells, span_y), F32)
    for s in range(2):
        ye = (span_y - 1) if s == 0 else 0
        for j, d in enumerate(YD[s]):
            pack = jnp.where(lane == 8 * s + j, relaxed[d, :, ye : ye + 1], pack)
    pack_t = pack.T
    for s in range(2):
        sendy[s] = pack_t[8 * s : 8 * s + 8, :]

    pl.semaphore_wait(barrier, owners - 1 + len(others))

    def motion_copy(o, slot):
        return pltpu.make_async_remote_copy(
            src_ref=motion_own, dst_ref=motion_all.at[slot], send_sem=ms.at[o], recv_sem=mr.at[slot],
            device_id=peer_of(o)[1], device_id_type=pl.DeviceIdType.MESH,
        )

    loop(1, owners, lambda o: motion_copy(o, me).start())

    halo = []

    def rim(src, dst, target):
        k = len(halo)
        c = pltpu.make_async_remote_copy(
            src_ref=src, dst_ref=dst, send_sem=hs.at[k], recv_sem=hr.at[k],
            device_id=target, device_id_type=pl.DeviceIdType.MESH,
        )
        c.start()
        halo.append(c)

    for s in range(2):
        xt, yt = (ap, bp) if s == 0 else (am, bm)
        rim(sendx.at[s], xin.at[s], dev(xt, b, e))
        rim(sende.at[s], ein.at[s], dev(xt, b, oe))
        rim(sendy.at[s], yin.at[s, 0], dev(a, yt, e))
        rim(sendy.at[s], yin.at[s, 1], dev(ap, yt, e))
        rim(sendy.at[s], yin.at[s, 2], dev(am, yt, e))
        rim(sendy.at[s], yin.at[s, 3], dev(a, yt, oe))
    rim(sendz, zin, dev(a, b, oe))

    for k in (0, 1, 2, 3, 4, 5, 6, 9, 10):
        small_in[k].wait()

    cell = lcell[0, 0]
    dirs = ldir[0, 0]
    row_of = cell // span_y
    lane_of = cell - row_of * span_y
    dirs_f = dirs.astype(F32)
    iota_c = lax.broadcasted_iota(jnp.int32, (cells, links), 0)
    iota_y = lax.broadcasted_iota(jnp.int32, (span_y, links), 0)
    row_t = jnp.where(iota_c == row_of, 1.0, 0.0).astype(BF16)
    lane_mask = iota_y == lane_of
    dmap[...] = dot(row_t, jnp.where(lane_mask, dirs_f, 0.0).astype(BF16), 1, 1)
    dm = dmap[...]
    post_map = jnp.zeros((cells, span_y), F32)
    for d in range(1, 19):
        post_map = jnp.where(dm == float(d), relaxed[d], post_map)
    picked = None
    for part in split3(post_map):
        t = dot(part.astype(BF16), row_t, 0, 0)
        picked = t if picked is None else picked + t
    post = jnp.sum(jnp.where(lane_mask, picked, 0.0), axis=0, keepdims=True)
    iota_s = lax.broadcasted_iota(jnp.int32, (slots, links), 0)
    slot_t = jnp.where(iota_s == lslot[0, 0], 1.0, 0.0).astype(BF16)

    vel = []
    for c in range(3):
        v = jnp.zeros((1, links), F32)
        for d in range(1, 19):
            if VEL[d][c]:
                v = jnp.where(dirs == d, float(VEL[d][c]), v)
        vel.append(v)
    six_w = jnp.where(dirs > 6, 6.0 * WT[7], 6.0 * WT[1])

    def motion_wait(o):
        p, _ = peer_of(o)
        motion_copy(o, p).wait_recv()

    loop(1, owners, motion_wait)
    bodies = bb_ref[0, 0]
    iota_b = lax.broadcasted_iota(jnp.int32, (body_own, slots), 0)

    def owner_onehot(o):
        return jnp.where(iota_b == bodies - o * body_own, 1.0, 0.0).astype(BF16)

    owner_of = bodies // body_own
    local_of = jnp.broadcast_to(bodies - owner_of * body_own, (8, slots))

    def gather(o, acc):
        g = jnp.take_along_axis(motion_all[o], local_of, axis=1)
        return jnp.where(owner_of == o, g, acc)

    slot_motion = lax.fori_loop(0, owners, gather, jnp.zeros((8, slots), F32), unroll=unroll)
    m = unstacked(dot(stacked(slot_motion), slot_t, 1, 0))
    mv = [m[i : i + 1, :] for i in range(6)]
    arm = [larm[i, 0, 0] for i in range(3)]
    wall = [
        mv[0] + mv[4] * arm[2] - mv[5] * arm[1],
        mv[1] + mv[5] * arm[0] - mv[3] * arm[2],
        mv[2] + mv[3] * arm[1] - mv[4] * arm[0],
    ]
    drop = six_w * (vel[0] * wall[0] + vel[1] * wall[1] + vel[2] * wall[2])
    bounce = post - drop
    live = jnp.where(dirs > 0, 1.0, 0.0)
    exchanged = (post + bounce) * live
    force = [vel[c] * exchanged for c in range(3)]
    torque = [
        arm[1] * force[2] - arm[2] * force[1],
        arm[2] * force[0] - arm[0] * force[2],
        arm[0] * force[1] - arm[1] * force[0],
    ]
    loads = jnp.concatenate(force + torque + [jnp.zeros((2, links), F32)], 0)
    slot_load = unstacked(dot(stacked(loads), slot_t, 1, 1))
    slot_parts = stacked(slot_load)

    def spread(o):
        tiles[o] = unstacked(dot(slot_parts, owner_onehot(o), 1, 1))

    loop(0, owners, spread)

    def force_copy(o, src, slot):
        return pltpu.make_async_remote_copy(
            src_ref=tiles.at[src], dst_ref=force_all.at[slot], send_sem=fs.at[o], recv_sem=fr.at[slot],
            device_id=peer_of(o)[1], device_id_type=pl.DeviceIdType.MESH,
        )

    loop(1, owners, lambda o: force_copy(o, peer_of(o)[0], me).start())
    force_all[me] = tiles[me]

    wm = None
    for part in split3(drop):
        t = dot(row_t, jnp.where(lane_mask, part, 0.0).astype(BF16), 1, 1)
        wm = t if wm is None else wm + t
    wmap[...] = wm

    for c in halo:
        c.wait_recv()
    lane_c = lax.broadcasted_iota(jnp.int32, (8, cells), 1)
    z_c = lane_c - (lane_c // span_z) * span_z
    sub_c = lax.broadcasted_iota(jnp.int32, (8, cells), 0)
    both = []
    for s in range(2):
        t0, t1, t2, t3 = (yin[s, k] for k in range(4))
        out = t0
        for j, d in enumerate(YD[s]):
            cx, _, cz = VEL[d]
            if cx == 1:
                v = jnp.where(lane_c < span_z, pltpu.roll(t1, span_z, 1), pltpu.roll(t0, span_z, 1))
            elif cx == -1:
                v = jnp.where(
                    lane_c >= cells - span_z,
                    pltpu.roll(t2, cells - span_z, 1),
                    pltpu.roll(t0, cells - span_z, 1),
                )
            elif cz == 1:
                v = jnp.where(z_c == 0, pltpu.roll(t3, cells - span_z + 1, 1), pltpu.roll(t0, 1, 1))
            elif cz == -1:
                v = jnp.where(
                    z_c == span_z - 1, pltpu.roll(t3, span_z - 1, 1), pltpu.roll(t0, cells - 1, 1)
                )
            else:
                continue
            out = jnp.where(sub_c == j, v, out)
        both.append(out)
    both.append(jnp.zeros((span_y - 16, cells), F32))
    ycols[...] = jnp.concatenate(both, 0).T

    iz = lax.broadcasted_iota(jnp.int32, (span_z, span_y), 0)
    iy = lax.broadcasted_iota(jnp.int32, (span_z, span_y), 1)
    for x in range(span_x):
        rows = slice(x * span_z, (x + 1) * span_z)
        dm_x = dmap[rows, :]
        wm_x = wmap[rows, :]
        for i in range(19):
            cx, cy, cz = VEL[i]
            sx = x - cx
            inside = 0 <= sx < span_x
            if inside:
                v = relaxed[i, sx * span_z : (sx + 1) * span_z, :]
            else:
                s = 0 if cx > 0 else 1
                v = xin[s, XD[s].index(i)]
            if cz:
                s = 0 if cz > 0 else 1
                if inside:
                    edge = zin[s, ZD[s].index(i), sx : sx + 1, :]
                else:
                    sxx = 0 if cx > 0 else 1
                    j = XZD[sxx].index(i)
                    edge = ein[sxx, j : j + 1, :]
                v = pltpu.roll(v, 1 if cz > 0 else span_z - 1, 0)
                v = jnp.where(iz == (0 if cz > 0 else span_z - 1), edge, v)
            if cy:
                s = 0 if cy > 0 else 1
                j = 8 * s + YD[s].index(i)
                v = pltpu.roll(v, 1 if cy > 0 else span_y - 1, 1)
                v = jnp.where(iy == (0 if cy > 0 else span_y - 1), ycols[rows, j : j + 1], v)
            if i:
                d = OPP[i]
                v = jnp.where(dm_x == float(d), relaxed[d, rows, :] - wm_x, v)
            nxt[i, x] = v

    def force_wait(o):
        p, _ = peer_of(o)
        force_copy(o, p, p).wait_recv()

    loop(1, owners, force_wait)
    half[...] = lax.fori_loop(
        0, owners, lambda o, acc: acc + force_all[o], jnp.zeros(half.shape, F32), unroll=unroll
    )
    swap = pltpu.make_async_remote_copy(
        src_ref=half, dst_ref=half_in, send_sem=cs, recv_sem=cr,
        device_id=dev(a, b, oe), device_id_type=pl.DeviceIdType.MESH,
    )
    swap.start()

    def sent(o):
        motion_copy(o, me).wait_send()
        force_copy(o, peer_of(o)[0], me).wait_send()

    loop(1, owners, sent)
    for c in halo:
        c.wait_send()
    swap.wait()
    load = half[...] + half_in[...]
    f = [load[i : i + 1, :] for i in range(6)]
    pos = [bpos[i : i + 1, :] for i in range(3)]
    qw, qx, qy, qz = (bquat[i : i + 1, :] for i in range(4))
    velo = [bvel[i : i + 1, :] + imass[...] * f[i] for i in range(3)]
    velo[2] = velo[2] - GRAV
    rot = [
        [1.0 - 2.0 * (qy * qy + qz * qz), 2.0 * (qx * qy - qw * qz), 2.0 * (qx * qz + qw * qy)],
        [2.0 * (qx * qy + qw * qz), 1.0 - 2.0 * (qx * qx + qz * qz), 2.0 * (qy * qz - qw * qx)],
        [2.0 * (qx * qz - qw * qy), 2.0 * (qy * qz + qw * qx), 1.0 - 2.0 * (qx * qx + qy * qy)],
    ]
    tq = f[3:6]
    acc = [
        iinert[c : c + 1, :] * (rot[0][c] * tq[0] + rot[1][c] * tq[1] + rot[2][c] * tq[2])
        for c in range(3)
    ]
    spin = [
        bspin[r : r + 1, :] + (rot[r][0] * acc[0] + rot[r][1] * acc[1] + rot[r][2] * acc[2])
        for r in range(3)
    ]
    sx, sy, sz = spin
    dq = [
        -(sx * qx + sy * qy + sz * qz),
        sx * qw + sy * qz - sz * qy,
        sy * qw + sz * qx - sx * qz,
        sz * qw + sx * qy - sy * qx,
    ]
    scale = lax.rsqrt(1.0 + 0.25 * (sx * sx + sy * sy + sz * sz))
    quat = [(q + 0.5 * k) * scale for q, k in zip((qw, qx, qy, qz), dq)]
    result = [pos[i] + velo[i] for i in range(3)] + quat + velo + spin
    for i, v in enumerate(result):
        bnext[i : i + 1, :] = v


def write_out(a, b, a_out, b_out, sems):
    copies = [pltpu.make_async_copy(a, a_out, sems.at[0]), pltpu.make_async_copy(b, b_out, sems.at[1])]
    for c in copies:
        c.start()
    for c in copies:
        c.wait()


def shards(sizes, *args):
    pop = args[0]
    span_x, span_z, span_y = pop.shape[1:]
    cells = span_x * span_z
    body_own = args[6].shape[1]
    owners = sizes[0] * sizes[1]
    args = list(args)
    args[10] = args[10].reshape(1, -1)
    vm = pl.BlockSpec(memory_space=pltpu.VMEM)
    dma = pltpu.SemaphoreType.DMA
    V = lambda *s: pltpu.VMEM(s, F32)
    args = [pltpu.with_memory_space_constraint(v, pltpu.MemorySpace.HBM) for v in args]
    hbm = pl.BlockSpec(memory_space=pltpu.MemorySpace.HBM)
    outs = pl.pallas_call(
        functools.partial(kernel, sizes),
        out_shape=(
            jax.ShapeDtypeStruct(pop.shape, F32),
            jax.ShapeDtypeStruct((13, body_own), F32),
        ),
        in_specs=[hbm] * len(args),
        out_specs=(vm, vm),
        scratch_shapes=[
            *[pltpu.VMEM(v.shape, v.dtype) for v in args],
            V(19, cells, span_y),
            V(2, 5, span_z, span_y), V(2, 5, span_z, span_y),
            V(2, 5, span_x, span_y), V(2, 5, span_x, span_y),
            V(2, 8, span_y), V(2, 8, span_y),
            V(2, 8, cells), V(2, 4, 8, cells),
            V(16, cells), V(cells, span_y),
            V(cells, span_y), V(cells, span_y),
            V(8, body_own), V(owners, 8, body_own),
            V(owners, 8, body_own), V(owners, 8, body_own),
            V(8, body_own), V(8, body_own),
            dma((13,)), dma((13,)),
            dma((owners,)), dma((owners,)),
            dma((owners,)), dma((owners,)),
            dma, dma,
            dma((POP_CHUNKS,)), dma((11,)),
        ],
        compiler_params=pltpu.CompilerParams(
            collective_id=0, has_side_effects=True, vmem_limit_bytes=K1_VMEM
        ),
        name="lattice_step",
    )(*args)
    return pl.pallas_call(
        write_out,
        out_shape=tuple(jax.ShapeDtypeStruct(v.shape, F32) for v in outs),
        in_specs=[vm, vm],
        out_specs=(hbm, hbm),
        scratch_shapes=[dma((2,))],
        compiler_params=pltpu.CompilerParams(vmem_limit_bytes=K2_VMEM),
        name="write_out",
    )(*outs)


def solution(mesh):
    sizes = (mesh.shape["gx"], mesh.shape["gy"])
    link = P("gx", "gz", "gy", None)
    body = P(None, ("gx", "gy"))
    return jax.shard_map(
        functools.partial(shards, sizes),
        mesh=mesh,
        in_specs=(
            P(None, "gx", "gz", "gy"), link, link, link, P(None, "gx", "gz", "gy", None), link,
            body, body, body, body, P(("gx", "gy")), body,
        ),
        out_specs=(P(None, "gx", "gz", "gy"), body),
        check_vma=False,
    )
```

```python
import functools

import jax
import jax.numpy as jnp
import numpy as np
from jax import lax
from jax.experimental import pallas as pl
from jax.experimental.pallas import tpu as pltpu
from jax.sharding import PartitionSpec as P

VEL = [
    (0, 0, 0), (1, 0, 0), (-1, 0, 0), (0, 1, 0), (0, -1, 0), (0, 0, 1), (0, 0, -1),
    (1, 1, 0), (-1, -1, 0), (1, -1, 0), (-1, 1, 0), (1, 0, 1), (-1, 0, -1), (1, 0, -1),
    (-1, 0, 1), (0, 1, 1), (0, -1, -1), (0, 1, -1), (0, -1, 1),
]
WT = [1.0 / 3.0] + [1.0 / 18.0] * 6 + [1.0 / 36.0] * 12
OPP = [0, 2, 1, 4, 3, 6, 5, 8, 7, 10, 9, 12, 11, 14, 13, 16, 15, 18, 17]
OMEGA = 1.25
POP_CHUNKS = 4
K1_VMEM = 24 * 1024 * 1024
K2_VMEM = 4 * 1024 * 1024
GRAV = 0.02
F32 = jnp.float32
BF16 = jnp.bfloat16
I32 = jnp.int32
SUB = 8
PAIRS = [(i, j) for i in range(6) for j in range(i, 6)]
NA = 6
NM = len(PAIRS)
NM_PAD = 24


def dirs_of(comp, sign):
    return [d for d in range(19) if VEL[d][comp] == sign]


XD = (dirs_of(0, 1), dirs_of(0, -1))
YD = (dirs_of(1, 1), dirs_of(1, -1))
ZD = (dirs_of(2, 1), dirs_of(2, -1))
XZD = tuple([d for d in XD[s] if VEL[d][2] != 0] for s in range(2))


def dot(a, b, ca, cb):
    return lax.dot_general(a, b, (((ca,), (cb,)), ((), ())), preferred_element_type=F32)


def stacked(v):
    hi = v.astype(BF16).astype(F32)
    return jnp.concatenate([hi, v - hi], 0).astype(BF16)


def unstacked(v):
    k = v.shape[0] // 2
    return v[0:k] + v[k : 2 * k]


def pick(table, index):
    index = jnp.clip(index, 0, table.shape[1] - 1)
    return jnp.take_along_axis(table, index, axis=1, mode="promise_in_bounds")


def spread(row, like):
    return jnp.broadcast_to(row, like.shape)


def kernel(
    sizes,
    pop_h, *rest,
):
    small_h, outs, rest = rest[:11], rest[11:15], rest[15:]
    pop, small, rest = rest[0], rest[1:12], rest[12:]
    step(sizes, pop_h, small_h, pop, *small, *outs, *rest)


def step(
    sizes, pop_h, small_h,
    pop, lcell, ldir, lslot, larm, bb_ref, bpos, bquat, bvel, bspin, imass, iinert,
    nxt, state, got_m, got_a,
    relaxed, sendx, xin, sendz, zin, sende, ein, sendy, yin, ycols,
    post_map, dmap, links_f, comps_m, comps_a, place_hot, row_hot, slot_m, slot_a,
    motion_own, motion_all, send_m, recv_m, send_a, recv_a,
    hs, xr, er, yr, zr, ms, mr, rs, rr, fs, fr, ps, ss,
):
    ngx, ngy, cap = sizes
    owners = ngx * ngy
    devices = 2 * owners
    span_x, span_z, span_y = pop.shape[1:]
    cells = span_x * span_z
    body_own = bvel.shape[1]
    slots = bb_ref.shape[-1]
    chunks = lcell.shape[0]
    per_row = slots // cap
    m_rows = recv_m.shape[1] - 1
    a, b, e = lax.axis_index("gx"), lax.axis_index("gy"), lax.axis_index("gz")
    me = a * ngy + b
    own = me * 2 + e
    ap, am = lax.rem(a + 1, ngx), lax.rem(a + ngx - 1, ngx)
    bp, bm = lax.rem(b + 1, ngy), lax.rem(b + ngy - 1, ngy)
    oe = 1 - e

    def dev(x, y, z):
        return {"gx": x, "gy": y, "gz": z}

    def peer_of(offset, z):
        p = lax.rem(me + offset, owners)
        return p, dev(p // ngy, lax.rem(p, ngy), z)

    unroll = owners <= 16

    def loop(lo, hi, body):
        if unroll:
            for i in range(lo, hi):
                body(i)
        else:
            pl.loop(lo, hi)(body)

    def remote(src, dst, send_sem, recv_sem, target):
        return pltpu.make_async_remote_copy(
            src_ref=src, dst_ref=dst, send_sem=send_sem, recv_sem=recv_sem,
            device_id=target, device_id_type=pl.DeviceIdType.MESH,
        )

    def wait_bytes(ref, sem):
        pltpu.make_async_copy(ref, ref, sem).wait()

    small = (lcell, ldir, lslot, larm, bb_ref, bpos, bquat, bvel, bspin, imass, iinert)
    small_in = [
        pltpu.make_async_copy(src, dst, ss.at[k]) for k, (src, dst) in enumerate(zip(small_h, small))
    ]
    chunk = span_x // POP_CHUNKS
    pop_in = [
        pltpu.make_async_copy(
            pop_h.at[:, pl.ds(k * chunk, chunk)], pop.at[:, pl.ds(k * chunk, chunk)], ps.at[k]
        )
        for k in range(POP_CHUNKS)
    ]
    for k in (4, 0, 1, 2, 3):
        small_in[k].start()
    for c in pop_in:
        c.start()
    for k in (7, 8, 5, 6, 9, 10):
        small_in[k].start()

    barrier = pltpu.get_barrier_semaphore()

    def greet(o):
        for z in (e, oe):
            pl.semaphore_signal(
                barrier, inc=1, device_id=peer_of(o, z)[1], device_id_type=pl.DeviceIdType.MESH
            )

    loop(1, owners, greet)
    pl.semaphore_signal(
        barrier, inc=1, device_id=dev(a, b, oe), device_id_type=pl.DeviceIdType.MESH
    )

    tile = (SUB, span_y)
    lane_t = lax.broadcasted_iota(I32, tile, 1)
    sub_t = lax.broadcasted_iota(I32, tile, 0)

    small_in[4].wait()
    bodies = bb_ref[...]
    owner_row = bodies // body_own
    local_row = bodies - owner_row * body_own
    sq = (slots, slots)
    owner_b = jnp.broadcast_to(owner_row.astype(F32), sq)
    iota_0 = lax.broadcasted_iota(I32, sq, 0)
    iota_1 = lax.broadcasted_iota(I32, sq, 1)
    earlier = jnp.where((owner_b == owner_b.T) & (iota_0 < iota_1), 1.0, 0.0)
    rank_row = jnp.sum(earlier, axis=0, keepdims=True)
    iota_o = lax.broadcasted_iota(I32, (owners, slots), 0)
    owned = iota_o == owner_row
    by_owner = jnp.where(owned, rank_row + 1.0, 0.0).astype(BF16)
    place = jnp.where(iota_0 == local_row, 1.0, 0.0).astype(BF16)
    rank_of = dot(by_owner, place, 1, 1)
    place_row = owner_row * cap + rank_row.astype(I32)
    for o in range(owners):
        send_m[o, m_rows : m_rows + 1, :] = rank_of[o : o + 1, :]
    lane_block = lane_t // cap
    unpack = sub_t * cap + lane_t - lane_block * cap

    def pack(src, count, dst):
        for g in range(owners // SUB):
            first = g * SUB * cap
            half = slice(first // slots * slots, first // slots * slots + slots)
            index = unpack + first % slots
            for r in range(-(-count // per_row)):
                out = jnp.zeros(tile, F32)
                for k in range(min(per_row, count - r * per_row)):
                    c = r * per_row + k
                    got = pick(spread(src[c : c + 1, half], out), index)
                    out = jnp.where(lane_block == k, got, out)
                for s in range(SUB):
                    dst[g * SUB + s, r : r + 1, :] = out[s : s + 1, :]

    for k in (0, 1, 2, 3):
        small_in[k].wait()
    cell = lcell[...]
    dirs = ldir[...]
    slot = lslot[...]
    row_of = cell // span_y
    lane_of = cell - row_of * span_y
    vel = []
    for c in range(3):
        v = jnp.zeros(tile, F32)
        for d in range(1, 19):
            if VEL[d][c]:
                v = jnp.where(dirs == d, float(VEL[d][c]), v)
        vel.append(v)
    six_w = jnp.where(dirs > 6, 6.0 * WT[7], 6.0 * WT[1])
    arm = [larm[SUB * i : SUB * (i + 1), :] for i in range(3)]
    f6 = vel + [
        arm[1] * vel[2] - arm[2] * vel[1],
        arm[2] * vel[0] - arm[0] * vel[2],
        arm[0] * vel[1] - arm[1] * vel[0],
    ]
    for q in range(6):
        links_f[q] = f6[q]
    links_f[6] = six_w
    wf = [six_w * v for v in f6]

    def by_chunk(comps, q, value):
        for j in range(chunks):
            comps[j, q : q + 1, :] = value[j : j + 1, :]

    for q, (i, j) in enumerate(PAIRS):
        by_chunk(comps_m, q, wf[i] * f6[j])
    for j in range(chunks):
        comps_m[j, NM:NM_PAD, :] = jnp.zeros((NM_PAD - NM, span_y), F32)
        comps_a[j, NA:SUB, :] = jnp.zeros((SUB - NA, span_y), F32)
    link_place = pick(spread(place_row, slot), slot)
    iota_p = lax.broadcasted_iota(I32, (owners * cap, span_y), 0)
    for j in range(chunks):
        place_hot[:, j * span_y : (j + 1) * span_y] = jnp.where(
            iota_p == link_place[j : j + 1, :], 1.0, 0.0
        ).astype(BF16)

    def slot_sums(comps):
        v = jnp.concatenate([comps[j] for j in range(chunks)], 1)
        return unstacked(dot(stacked(v), place_hot[...], 1, 1))

    slot_m[...] = slot_sums(comps_m)
    pack(slot_m, NM, send_m)

    iota_c = lax.broadcasted_iota(I32, (cells, span_y), 0)
    iota_y = lax.broadcasted_iota(I32, (span_y, span_y), 0)

    def at_lanes(value):
        return jnp.concatenate(
            [
                jnp.where(iota_y == lane_of[j : j + 1, :], value[j : j + 1, :], 0.0).astype(BF16)
                for j in range(chunks)
            ],
            1,
        )

    for j in range(chunks):
        row_hot[:, j * span_y : (j + 1) * span_y] = jnp.where(
            iota_c == row_of[j : j + 1, :], 1.0, 0.0
        ).astype(BF16)
    dmap[...] = dot(row_hot[...], at_lanes(dirs.astype(F32)), 1, 1).astype(I32)

    for x in range(span_x):
        if x % chunk == 0:
            pop_in[x // chunk].wait()
        for z in range(0, span_z, SUB):
            f = [pop[d, x, z : z + SUB, :] for d in range(19)]
            rho = f[0]
            for d in range(1, 19):
                rho = rho + f[d]
            inv = 1.0 / rho
            u = []
            for c in range(3):
                pos, neg = dirs_of(c, 1), dirs_of(c, -1)
                tot = f[pos[0]] - f[neg[0]]
                for p, q in zip(pos[1:], neg[1:]):
                    tot = tot + (f[p] - f[q])
                u.append(tot * inv)
            usq = 1.0 - 1.5 * (u[0] * u[0] + u[1] * u[1] + u[2] * u[2])
            rows = pl.ds(x * span_z + z, SUB)
            keep = 1.0 - OMEGA
            relaxed[0, rows, :] = keep * f[0] + (OMEGA * WT[0]) * rho * usq
            at = dmap[rows, :]
            post = jnp.zeros(tile, F32)
            for d in range(1, 19, 2):
                terms = [u[c] if VEL[d][c] > 0 else -u[c] for c in range(3) if VEL[d][c]]
                proj = terms[0] if len(terms) == 1 else terms[0] + terms[1]
                scale = (OMEGA * WT[d]) * rho
                even = scale * (usq + 4.5 * proj * proj)
                odd = scale * (3.0 * proj)
                v = keep * f[d] + (even + odd)
                relaxed[d, rows, :] = v
                post = jnp.where(at == d, v, post)
                v = keep * f[d + 1] + (even - odd)
                relaxed[d + 1, rows, :] = v
                post = jnp.where(at == d + 1, v, post)
            post_map[rows, :] = post

    lane = lax.broadcasted_iota(I32, (cells, span_y), 1)
    packed = jnp.zeros((cells, span_y), F32)
    for s in range(2):
        ye = (span_y - 1) if s == 0 else 0
        for j, d in enumerate(YD[s]):
            packed = jnp.where(lane == 8 * s + j, relaxed[d, :, ye : ye + 1], packed)
    pack_t = packed.T
    for s in range(2):
        sendy[s] = pack_t[8 * s : 8 * s + 8, :]
    for s in range(2):
        xe = (span_x - 1) if s == 0 else 0
        ze = (span_z - 1) if s == 0 else 0
        for j, d in enumerate(XD[s]):
            sendx[s, j] = relaxed[d, xe * span_z : (xe + 1) * span_z, :]
        for j, d in enumerate(ZD[s]):
            for x in range(span_x):
                r = x * span_z + ze
                sendz[s, j, x : x + 1, :] = relaxed[d, r : r + 1, :]
        sende[s] = jnp.zeros(sende.shape[1:], F32)
        for j, d in enumerate(XZD[s]):
            r = xe * span_z + ((span_z - 1) if VEL[d][2] > 0 else 0)
            sende[s, j : j + 1, :] = relaxed[d, r : r + 1, :]

    small_in[7].wait()
    small_in[8].wait()
    motion_own[...] = jnp.concatenate(
        [bvel[...], bspin[...], jnp.zeros((2, body_own), F32)], 0
    )
    motion_all[me] = motion_own[...]
    recv_m[own] = send_m[me]

    pl.semaphore_wait(barrier, devices - 1)

    for s in range(2):
        xt, yt = (ap, bp) if s == 0 else (am, bm)
        for k, t in enumerate((dev(a, yt, e), dev(ap, yt, e), dev(am, yt, e), dev(a, yt, oe))):
            remote(sendy.at[s], yin.at[s, k], hs, yr, t).start()
        remote(sendx.at[s], xin.at[s], hs, xr, dev(xt, b, e)).start()
        remote(sende.at[s], ein.at[s], hs, er, dev(xt, b, oe)).start()
    remote(sendz, zin, hs, zr, dev(a, b, oe)).start()

    def send_motion(o):
        remote(motion_own, motion_all.at[me], ms, mr, peer_of(o, e)[1]).start()

    loop(1, owners, send_motion)

    def send_response(o):
        for z in (e, oe):
            p, target = peer_of(o, z)
            remote(send_m.at[p], recv_m.at[own], rs, rr, target).start()

    loop(1, owners, send_response)
    remote(send_m.at[me], recv_m.at[own], rs, rr, dev(a, b, oe)).start()

    parts = [jnp.zeros(tile, F32) for _ in range(4)]
    for r in range(cells):
        got = pick(spread(post_map[r : r + 1, :], parts[0]), lane_of)
        parts[r % 4] = jnp.where(row_of == r, got, parts[r % 4])
    post2 = 2.0 * ((parts[0] + parts[1]) + (parts[2] + parts[3]))
    for q in range(NA):
        by_chunk(comps_a, q, post2 * links_f[q])
    slot_a[...] = slot_sums(comps_a)
    pack(slot_a, NA, send_a)
    recv_a[own] = send_a[me]

    def send_push(o):
        for z in (e, oe):
            p, target = peer_of(o, z)
            remote(send_a.at[p], recv_a.at[own], fs, fr, target).start()

    loop(1, owners, send_push)
    remote(send_a.at[me], recv_a.at[own], fs, fr, dev(a, b, oe)).start()

    for k in (5, 6, 9, 10):
        small_in[k].wait()
    wait_bytes(xin, xr)
    wait_bytes(ein, er)
    wait_bytes(zin, zr)
    iz = lax.broadcasted_iota(I32, (span_z, span_y), 0)
    iy = lax.broadcasted_iota(I32, (span_z, span_y), 1)
    for x in range(span_x):
        for i in range(19):
            cx, cy, cz = VEL[i]
            sx = x - cx
            inside = 0 <= sx < span_x
            if inside:
                v = relaxed[i, sx * span_z : (sx + 1) * span_z, :]
            else:
                s = 0 if cx > 0 else 1
                v = xin[s, XD[s].index(i)]
            if cz:
                s = 0 if cz > 0 else 1
                if inside:
                    edge = zin[s, ZD[s].index(i), sx : sx + 1, :]
                else:
                    sxx = 0 if cx > 0 else 1
                    j = XZD[sxx].index(i)
                    edge = ein[sxx, j : j + 1, :]
                v = pltpu.roll(v, 1 if cz > 0 else span_z - 1, 0)
                v = jnp.where(iz == (0 if cz > 0 else span_z - 1), edge, v)
            if cy:
                v = pltpu.roll(v, 1 if cy > 0 else span_y - 1, 1)
            nxt[i, x] = v

    state[0:16, :] = jnp.concatenate(
        [bpos[...], bquat[...], bvel[...], bspin[...], iinert[...]], 0
    )
    state[16:17, :] = imass[...]

    wait_bytes(motion_all.at[pl.ds(0, owners - 1)], mr)
    local_b = spread(local_row, lane_t)

    def gather_motion(o, acc):
        return jnp.where(owner_row == o, pick(motion_all[o], local_b), acc)

    slot_motion = lax.fori_loop(0, owners, gather_motion, jnp.zeros(tile, F32), unroll=unroll)
    along = None
    for q in range(6):
        t = links_f[q] * pick(spread(slot_motion[q : q + 1, :], slot), slot)
        along = t if along is None else along + t
    drop = links_f[6] * along
    drop_hi = drop.astype(BF16).astype(F32)
    drops = jnp.concatenate([at_lanes(drop_hi), at_lanes(drop - drop_hi)], 0)
    wall = dot(row_hot[...], drops, 1, 1)
    post_map[...] = post_map[...] - (wall[:, 0:span_y] + wall[:, span_y : 2 * span_y])

    wait_bytes(yin, yr)
    lane_c = lax.broadcasted_iota(I32, (8, cells), 1)
    z_c = lane_c - (lane_c // span_z) * span_z
    sub_c = lax.broadcasted_iota(I32, (8, cells), 0)
    both = []
    for s in range(2):
        t0, t1, t2, t3 = (yin[s, k] for k in range(4))
        out = t0
        for j, d in enumerate(YD[s]):
            cx, _, cz = VEL[d]
            if cx == 1:
                v = jnp.where(lane_c < span_z, pltpu.roll(t1, span_z, 1), pltpu.roll(t0, span_z, 1))
            elif cx == -1:
                v = jnp.where(
                    lane_c >= cells - span_z,
                    pltpu.roll(t2, cells - span_z, 1),
                    pltpu.roll(t0, cells - span_z, 1),
                )
            elif cz == 1:
                v = jnp.where(z_c == 0, pltpu.roll(t3, cells - span_z + 1, 1), pltpu.roll(t0, 1, 1))
            elif cz == -1:
                v = jnp.where(
                    z_c == span_z - 1, pltpu.roll(t3, span_z - 1, 1), pltpu.roll(t0, cells - 1, 1)
                )
            else:
                continue
            out = jnp.where(sub_c == j, v, out)
        both.append(out)
    both.append(jnp.zeros((span_y - 16, cells), F32))
    ycols[...] = jnp.concatenate(both, 0).T

    for x in range(span_x):
        rows = slice(x * span_z, (x + 1) * span_z)
        at = dmap[rows, :]
        bounce = post_map[rows, :]
        for i in range(1, 19):
            cy = VEL[i][1]
            v = nxt[i, x]
            if cy:
                s = 0 if cy > 0 else 1
                j = 8 * s + YD[s].index(i)
                v = jnp.where(iy == (0 if cy > 0 else span_y - 1), ycols[rows, j : j + 1], v)
            nxt[i, x] = jnp.where(at == OPP[i], bounce, v)

    wait_bytes(sendx, hs)
    wait_bytes(sende, hs)
    wait_bytes(yin, hs)
    wait_bytes(sendz, hs)
    wait_bytes(motion_all.at[pl.ds(0, owners - 1)], ms)
    wait_bytes(recv_m.at[pl.ds(0, devices - 1)], rs)
    wait_bytes(recv_a.at[pl.ds(0, devices - 1)], fs)

    wait_bytes(recv_m.at[pl.ds(0, devices - 1)], rr)
    wait_bytes(recv_a.at[pl.ds(0, devices - 1)], fr)
    got_m[...] = recv_m[...]
    got_a[...] = recv_a[...]


def finish(cap, nxt, state, got_m, got_a, a_out, b_out, result, sems):
    out = pltpu.make_async_copy(nxt, a_out, sems.at[0])
    out.start()
    devices, slots = got_a.shape[0], got_a.shape[2]
    per_row = slots // cap
    m_rows = got_m.shape[1] - 1
    groups = NM_PAD // SUB
    sub_t = lax.broadcasted_iota(I32, (SUB, slots), 0)

    def gather(k, acc):
        rank = spread(got_m[k, m_rows : m_rows + 1, :], sub_t).astype(I32) - 1
        known = rank >= 0
        safe = sub_t * cap + jnp.clip(rank, 0, cap - 1)
        added = []
        for g in range(groups):
            r, base = (g * SUB) // per_row, (g * SUB) % per_row
            added.append(pick(spread(got_m[k, r : r + 1, :], safe), safe + base * cap))
        added.append(pick(spread(got_a[k], safe), safe))
        return tuple(v + jnp.where(known, w, 0.0) for v, w in zip(acc, added))

    zero = jnp.zeros((SUB, slots), F32)
    sums = lax.fori_loop(0, devices, gather, (zero,) * (groups + 1), unroll=devices <= 32)
    f = [sums[groups][i : i + 1, :] for i in range(6)]
    u = [state[7 + i : 8 + i, :] for i in range(6)]
    for q, (i, j) in enumerate(PAIRS):
        m = sums[q // SUB][q % SUB : q % SUB + 1, :]
        f[i] = f[i] - m * u[j]
        if i != j:
            f[j] = f[j] - m * u[i]
    pos = [state[i : i + 1, :] for i in range(3)]
    qw, qx, qy, qz = (state[3 + i : 4 + i, :] for i in range(4))
    vel, turn = u[0:3], u[3:6]
    inert = [state[13 + i : 14 + i, :] for i in range(3)]
    imass = state[16:17, :]
    velo = [vel[i] + imass * f[i] for i in range(3)]
    velo[2] = velo[2] - GRAV
    rot = [
        [1.0 - 2.0 * (qy * qy + qz * qz), 2.0 * (qx * qy - qw * qz), 2.0 * (qx * qz + qw * qy)],
        [2.0 * (qx * qy + qw * qz), 1.0 - 2.0 * (qx * qx + qz * qz), 2.0 * (qy * qz - qw * qx)],
        [2.0 * (qx * qz - qw * qy), 2.0 * (qy * qz + qw * qx), 1.0 - 2.0 * (qx * qx + qy * qy)],
    ]
    tq = f[3:6]
    acc = [
        inert[c] * (rot[0][c] * tq[0] + rot[1][c] * tq[1] + rot[2][c] * tq[2]) for c in range(3)
    ]
    spin = [
        turn[r] + (rot[r][0] * acc[0] + rot[r][1] * acc[1] + rot[r][2] * acc[2]) for r in range(3)
    ]
    sx, sy, sz = spin
    dq = [
        -(sx * qx + sy * qy + sz * qz),
        sx * qw + sy * qz - sz * qy,
        sy * qw + sz * qx - sx * qz,
        sz * qw + sx * qy - sy * qx,
    ]
    scale = lax.rsqrt(1.0 + 0.25 * (sx * sx + sy * sy + sz * sz))
    quat = [(q + 0.5 * k) * scale for q, k in zip((qw, qx, qy, qz), dq)]
    rows = [pos[i] + velo[i] for i in range(3)] + quat + velo + spin
    for i, v in enumerate(rows):
        result[i : i + 1, :] = v
    small = pltpu.make_async_copy(result, b_out, sems.at[1])
    small.start()
    small.wait()
    out.wait()


def shards(sizes, *args):
    pop = args[0]
    span_x, span_z, span_y = pop.shape[1:]
    cells = span_x * span_z
    body_own = args[6].shape[1]
    slots = args[5].shape[-1]
    links = args[1].shape[-1]
    chunks = links // span_y
    owners = sizes[0] * sizes[1]
    devices = 2 * owners
    cap = max(1, 2 * slots // owners)
    m_rows = -(-NM // (slots // cap))
    args = list(args)
    for k in (1, 2, 3):
        args[k] = args[k].reshape(chunks, span_y)
    args[4] = args[4].reshape(3 * chunks, span_y)
    args[5] = args[5].reshape(1, slots)
    args[10] = args[10].reshape(1, -1)
    vm = pl.BlockSpec(memory_space=pltpu.VMEM)
    dma = pltpu.SemaphoreType.DMA
    V = lambda *s: pltpu.VMEM(s, F32)
    VI = lambda *s: pltpu.VMEM(s, I32)
    args = [pltpu.with_memory_space_constraint(v, pltpu.MemorySpace.HBM) for v in args]
    hbm = pl.BlockSpec(memory_space=pltpu.MemorySpace.HBM)
    outs = pl.pallas_call(
        functools.partial(kernel, (sizes[0], sizes[1], cap)),
        out_shape=(
            jax.ShapeDtypeStruct(pop.shape, F32),
            jax.ShapeDtypeStruct((24, body_own), F32),
            jax.ShapeDtypeStruct((devices, m_rows + 1, slots), F32),
            jax.ShapeDtypeStruct((devices, 1, slots), F32),
        ),
        in_specs=[hbm] * len(args),
        out_specs=(vm,) * 4,
        scratch_shapes=[
            *[pltpu.VMEM(v.shape, v.dtype) for v in args],
            V(19, cells, span_y),
            V(2, 5, span_z, span_y), V(2, 5, span_z, span_y),
            V(2, 5, span_x, span_y), V(2, 5, span_x, span_y),
            V(2, 8, span_y), V(2, 8, span_y),
            V(2, 8, cells), V(2, 4, 8, cells),
            V(cells, span_y),
            V(cells, span_y), VI(cells, span_y),
            V(7, SUB, span_y), V(chunks, NM_PAD, span_y), V(chunks, SUB, span_y),
            pltpu.VMEM((owners * cap, links), BF16), pltpu.VMEM((cells, links), BF16),
            V(NM_PAD, owners * cap), V(SUB, owners * cap),
            V(8, body_own), V(owners, 8, body_own),
            V(owners, m_rows + 1, slots), V(devices, m_rows + 1, slots),
            V(owners, 1, slots), V(devices, 1, slots),
            *[dma] * 11,
            dma((POP_CHUNKS,)), dma((11,)),
        ],
        compiler_params=pltpu.CompilerParams(
            collective_id=0, has_side_effects=True, vmem_limit_bytes=K1_VMEM
        ),
        name="lattice_step",
    )(*args)
    return pl.pallas_call(
        functools.partial(finish, cap),
        out_shape=(
            jax.ShapeDtypeStruct(pop.shape, F32),
            jax.ShapeDtypeStruct((13, body_own), F32),
        ),
        in_specs=[vm] * 4,
        out_specs=(hbm, hbm),
        scratch_shapes=[V(13, body_own), dma((2,))],
        compiler_params=pltpu.CompilerParams(vmem_limit_bytes=K2_VMEM),
        name="finish",
    )(*outs)


def solution(mesh):
    sizes = (mesh.shape["gx"], mesh.shape["gy"])
    link = P("gx", "gz", "gy", None)
    body = P(None, ("gx", "gy"))
    return jax.shard_map(
        functools.partial(shards, sizes),
        mesh=mesh,
        in_specs=(
            P(None, "gx", "gz", "gy"), link, link, link, P(None, "gx", "gz", "gy", None), link,
            body, body, body, body, P(("gx", "gy")), body,
        ),
        out_specs=(P(None, "gx", "gz", "gy"), body),
        check_vma=False,
    )
```

```python
import functools

import jax
import jax.numpy as jnp
import numpy as np
from jax import lax
from jax.experimental import pallas as pl
from jax.experimental.pallas import tpu as pltpu
from jax.sharding import PartitionSpec as P

VEL = [
    (0, 0, 0), (1, 0, 0), (-1, 0, 0), (0, 1, 0), (0, -1, 0), (0, 0, 1), (0, 0, -1),
    (1, 1, 0), (-1, -1, 0), (1, -1, 0), (-1, 1, 0), (1, 0, 1), (-1, 0, -1), (1, 0, -1),
    (-1, 0, 1), (0, 1, 1), (0, -1, -1), (0, 1, -1), (0, -1, 1),
]
WT = [1.0 / 3.0] + [1.0 / 18.0] * 6 + [1.0 / 36.0] * 12
OPP = [0, 2, 1, 4, 3, 6, 5, 8, 7, 10, 9, 12, 11, 14, 13, 16, 15, 18, 17]
OMEGA = 1.25
POP_CHUNKS = 4
OUT_CHUNKS = 4
K1_VMEM = 24 * 1024 * 1024
K2_VMEM = 4 * 1024 * 1024
GRAV = 0.02
F32 = jnp.float32
BF16 = jnp.bfloat16
I32 = jnp.int32
SUB = 8
PAIRS = [(i, j) for i in range(6) for j in range(i, 6)]
NA = 6
NM = len(PAIRS)
NM_PAD = 24


def dirs_of(comp, sign):
    return [d for d in range(19) if VEL[d][comp] == sign]


XD = (dirs_of(0, 1), dirs_of(0, -1))
YD = (dirs_of(1, 1), dirs_of(1, -1))
ZD = (dirs_of(2, 1), dirs_of(2, -1))
XZD = tuple([d for d in XD[s] if VEL[d][2] != 0] for s in range(2))


def dot(a, b, ca, cb):
    return lax.dot_general(a, b, (((ca,), (cb,)), ((), ())), preferred_element_type=F32)


def stacked(v):
    hi = v.astype(BF16).astype(F32)
    return jnp.concatenate([hi, v - hi], 0).astype(BF16)


def unstacked(v):
    k = v.shape[0] // 2
    return v[0:k] + v[k : 2 * k]


def pick(table, index):
    index = jnp.clip(index, 0, table.shape[1] - 1)
    return jnp.take_along_axis(table, index, axis=1, mode="promise_in_bounds")


def spread(row, like):
    return jnp.broadcast_to(row, like.shape)


def kernel(
    sizes,
    pop_h, *rest,
):
    small_h, outs, rest = rest[:11], rest[11:18], rest[18:]
    pop, small, rest = rest[0], rest[1:12], rest[12:]
    step(sizes, pop_h, small_h, pop, *small, *outs, *rest)


def step(
    sizes, pop_h, small_h,
    pop, lcell, ldir, lslot, larm, bb_ref, bpos, bquat, bvel, bspin, imass, iinert,
    nxt, post_map, dmap, ycols, state, got_m, got_a,
    relaxed, sendx, xin, sendz, zin, sende, ein, sendy, yin,
    links_f, comps_m, comps_a, place_hot, row_hot, slot_m, slot_a,
    motion_own, motion_all, send_m, recv_m, send_a, recv_a,
    hs, xr, er, yr, zr, ms, mr, rs, rr, fs, fr, ps, ss,
):
    ngx, ngy, cap = sizes
    owners = ngx * ngy
    devices = 2 * owners
    span_x, span_z, span_y = pop.shape[1:]
    cells = span_x * span_z
    body_own = bvel.shape[1]
    slots = bb_ref.shape[-1]
    chunks = lcell.shape[0]
    per_row = slots // cap
    m_rows = recv_m.shape[1] - 1
    a, b, e = lax.axis_index("gx"), lax.axis_index("gy"), lax.axis_index("gz")
    me = a * ngy + b
    own = me * 2 + e
    ap, am = lax.rem(a + 1, ngx), lax.rem(a + ngx - 1, ngx)
    bp, bm = lax.rem(b + 1, ngy), lax.rem(b + ngy - 1, ngy)
    oe = 1 - e

    def dev(x, y, z):
        return {"gx": x, "gy": y, "gz": z}

    def peer_of(offset, z):
        p = lax.rem(me + offset, owners)
        return p, dev(p // ngy, lax.rem(p, ngy), z)

    unroll = owners <= 16

    def loop(lo, hi, body):
        if unroll:
            for i in range(lo, hi):
                body(i)
        else:
            pl.loop(lo, hi)(body)

    def remote(src, dst, send_sem, recv_sem, target):
        return pltpu.make_async_remote_copy(
            src_ref=src, dst_ref=dst, send_sem=send_sem, recv_sem=recv_sem,
            device_id=target, device_id_type=pl.DeviceIdType.MESH,
        )

    def wait_bytes(ref, sem):
        pltpu.make_async_copy(ref, ref, sem).wait()

    small = (lcell, ldir, lslot, larm, bb_ref, bpos, bquat, bvel, bspin, imass, iinert)
    small_in = [
        pltpu.make_async_copy(src, dst, ss.at[k]) for k, (src, dst) in enumerate(zip(small_h, small))
    ]
    chunk = span_x // POP_CHUNKS
    pop_in = [
        pltpu.make_async_copy(
            pop_h.at[:, pl.ds(k * chunk, chunk)], pop.at[:, pl.ds(k * chunk, chunk)], ps.at[k]
        )
        for k in range(POP_CHUNKS)
    ]
    for k in (4, 0, 1, 2, 3):
        small_in[k].start()
    for c in pop_in:
        c.start()
    for k in (7, 8, 5, 6, 9, 10):
        small_in[k].start()

    barrier = pltpu.get_barrier_semaphore()

    def greet(o):
        for z in (e, oe):
            pl.semaphore_signal(
                barrier, inc=1, device_id=peer_of(o, z)[1], device_id_type=pl.DeviceIdType.MESH
            )

    loop(1, owners, greet)
    pl.semaphore_signal(
        barrier, inc=1, device_id=dev(a, b, oe), device_id_type=pl.DeviceIdType.MESH
    )

    tile = (SUB, span_y)
    lane_t = lax.broadcasted_iota(I32, tile, 1)
    sub_t = lax.broadcasted_iota(I32, tile, 0)

    small_in[4].wait()
    bodies = bb_ref[...]
    owner_row = bodies // body_own
    local_row = bodies - owner_row * body_own
    sq = (slots, slots)
    owner_b = jnp.broadcast_to(owner_row.astype(F32), sq)
    iota_0 = lax.broadcasted_iota(I32, sq, 0)
    iota_1 = lax.broadcasted_iota(I32, sq, 1)
    earlier = jnp.where((owner_b == owner_b.T) & (iota_0 < iota_1), 1.0, 0.0)
    rank_row = jnp.sum(earlier, axis=0, keepdims=True)
    iota_o = lax.broadcasted_iota(I32, (owners, slots), 0)
    owned = iota_o == owner_row
    by_owner = jnp.where(owned, rank_row + 1.0, 0.0).astype(BF16)
    place = jnp.where(iota_0 == local_row, 1.0, 0.0).astype(BF16)
    rank_of = dot(by_owner, place, 1, 1)
    place_row = owner_row * cap + rank_row.astype(I32)
    for o in range(owners):
        send_m[o, m_rows : m_rows + 1, :] = rank_of[o : o + 1, :]
    lane_block = lane_t // cap
    unpack = sub_t * cap + lane_t - lane_block * cap

    def pack(src, count, dst):
        for g in range(owners // SUB):
            first = g * SUB * cap
            half = slice(first // slots * slots, first // slots * slots + slots)
            index = unpack + first % slots
            for r in range(-(-count // per_row)):
                out = jnp.zeros(tile, F32)
                for k in range(min(per_row, count - r * per_row)):
                    c = r * per_row + k
                    got = pick(spread(src[c : c + 1, half], out), index)
                    out = jnp.where(lane_block == k, got, out)
                for s in range(SUB):
                    dst[g * SUB + s, r : r + 1, :] = out[s : s + 1, :]

    for k in (0, 1, 2, 3):
        small_in[k].wait()
    cell = lcell[...]
    dirs = ldir[...]
    slot = lslot[...]
    row_of = cell // span_y
    lane_of = cell - row_of * span_y
    vel = []
    for c in range(3):
        v = jnp.zeros(tile, F32)
        for d in range(1, 19):
            if VEL[d][c]:
                v = jnp.where(dirs == d, float(VEL[d][c]), v)
        vel.append(v)
    six_w = jnp.where(dirs > 6, 6.0 * WT[7], 6.0 * WT[1])
    arm = [larm[SUB * i : SUB * (i + 1), :] for i in range(3)]
    f6 = vel + [
        arm[1] * vel[2] - arm[2] * vel[1],
        arm[2] * vel[0] - arm[0] * vel[2],
        arm[0] * vel[1] - arm[1] * vel[0],
    ]
    for q in range(6):
        links_f[q] = f6[q]
    links_f[6] = six_w
    wf = [six_w * v for v in f6]

    def by_chunk(comps, q, value):
        for j in range(chunks):
            comps[j, q : q + 1, :] = value[j : j + 1, :]

    for q, (i, j) in enumerate(PAIRS):
        by_chunk(comps_m, q, wf[i] * f6[j])
    for j in range(chunks):
        comps_m[j, NM:NM_PAD, :] = jnp.zeros((NM_PAD - NM, span_y), F32)
        comps_a[j, NA:SUB, :] = jnp.zeros((SUB - NA, span_y), F32)
    link_place = pick(spread(place_row, slot), slot)
    iota_p = lax.broadcasted_iota(I32, (owners * cap, span_y), 0)
    for j in range(chunks):
        place_hot[:, j * span_y : (j + 1) * span_y] = jnp.where(
            iota_p == link_place[j : j + 1, :], 1.0, 0.0
        ).astype(BF16)

    def slot_sums(comps):
        v = jnp.concatenate([comps[j] for j in range(chunks)], 1)
        return unstacked(dot(stacked(v), place_hot[...], 1, 1))

    slot_m[...] = slot_sums(comps_m)
    pack(slot_m, NM, send_m)

    iota_c = lax.broadcasted_iota(I32, (cells, span_y), 0)
    iota_y = lax.broadcasted_iota(I32, (span_y, span_y), 0)

    def at_lanes(value):
        return jnp.concatenate(
            [
                jnp.where(iota_y == lane_of[j : j + 1, :], value[j : j + 1, :], 0.0).astype(BF16)
                for j in range(chunks)
            ],
            1,
        )

    for j in range(chunks):
        row_hot[:, j * span_y : (j + 1) * span_y] = jnp.where(
            iota_c == row_of[j : j + 1, :], 1.0, 0.0
        ).astype(BF16)
    dmap[...] = dot(row_hot[...], at_lanes(dirs.astype(F32)), 1, 1).astype(I32)

    for x in range(span_x):
        if x % chunk == 0:
            pop_in[x // chunk].wait()
        for z in range(0, span_z, SUB):
            f = [pop[d, x, z : z + SUB, :] for d in range(19)]
            rho = f[0]
            for d in range(1, 19):
                rho = rho + f[d]
            inv = 1.0 / rho
            u = []
            for c in range(3):
                pos, neg = dirs_of(c, 1), dirs_of(c, -1)
                tot = f[pos[0]] - f[neg[0]]
                for p, q in zip(pos[1:], neg[1:]):
                    tot = tot + (f[p] - f[q])
                u.append(tot * inv)
            usq = 1.0 - 1.5 * (u[0] * u[0] + u[1] * u[1] + u[2] * u[2])
            rows = pl.ds(x * span_z + z, SUB)
            keep = 1.0 - OMEGA
            relaxed[0, rows, :] = keep * f[0] + (OMEGA * WT[0]) * rho * usq
            at = dmap[rows, :]
            post = jnp.zeros(tile, F32)
            for d in range(1, 19, 2):
                terms = [u[c] if VEL[d][c] > 0 else -u[c] for c in range(3) if VEL[d][c]]
                proj = terms[0] if len(terms) == 1 else terms[0] + terms[1]
                scale = (OMEGA * WT[d]) * rho
                even = scale * (usq + 4.5 * proj * proj)
                odd = scale * (3.0 * proj)
                v = keep * f[d] + (even + odd)
                relaxed[d, rows, :] = v
                post = jnp.where(at == d, v, post)
                v = keep * f[d + 1] + (even - odd)
                relaxed[d + 1, rows, :] = v
                post = jnp.where(at == d + 1, v, post)
            post_map[rows, :] = post

    lane = lax.broadcasted_iota(I32, (cells, span_y), 1)
    packed = jnp.zeros((cells, span_y), F32)
    for s in range(2):
        ye = (span_y - 1) if s == 0 else 0
        for j, d in enumerate(YD[s]):
            packed = jnp.where(lane == 8 * s + j, relaxed[d, :, ye : ye + 1], packed)
    pack_t = packed.T
    for s in range(2):
        sendy[s] = pack_t[8 * s : 8 * s + 8, :]
    for s in range(2):
        xe = (span_x - 1) if s == 0 else 0
        ze = (span_z - 1) if s == 0 else 0
        for j, d in enumerate(XD[s]):
            sendx[s, j] = relaxed[d, xe * span_z : (xe + 1) * span_z, :]
        for j, d in enumerate(ZD[s]):
            for x in range(span_x):
                r = x * span_z + ze
                sendz[s, j, x : x + 1, :] = relaxed[d, r : r + 1, :]
        sende[s] = jnp.zeros(sende.shape[1:], F32)
        for j, d in enumerate(XZD[s]):
            r = xe * span_z + ((span_z - 1) if VEL[d][2] > 0 else 0)
            sende[s, j : j + 1, :] = relaxed[d, r : r + 1, :]

    small_in[7].wait()
    small_in[8].wait()
    motion_own[...] = jnp.concatenate(
        [bvel[...], bspin[...], jnp.zeros((2, body_own), F32)], 0
    )
    motion_all[me] = motion_own[...]
    recv_m[own] = send_m[me]

    pl.semaphore_wait(barrier, devices - 1)

    remote(sendz, zin, hs, zr, dev(a, b, oe)).start()
    for s in range(2):
        xt, yt = (ap, bp) if s == 0 else (am, bm)
        for k, t in enumerate((dev(a, yt, e), dev(ap, yt, e), dev(am, yt, e), dev(a, yt, oe))):
            remote(sendy.at[s], yin.at[s, k], hs, yr, t).start()

    def send_motion(o):
        remote(motion_own, motion_all.at[me], ms, mr, peer_of(o, e)[1]).start()

    loop(1, owners, send_motion)

    for s in range(2):
        xt, yt = (ap, bp) if s == 0 else (am, bm)
        remote(sendx.at[s], xin.at[s], hs, xr, dev(xt, b, e)).start()
        remote(sende.at[s], ein.at[s], hs, er, dev(xt, b, oe)).start()

    def send_response(o):
        for z in (e, oe):
            p, target = peer_of(o, z)
            remote(send_m.at[p], recv_m.at[own], rs, rr, target).start()

    loop(1, owners, send_response)
    remote(send_m.at[me], recv_m.at[own], rs, rr, dev(a, b, oe)).start()

    parts = [jnp.zeros(tile, F32) for _ in range(4)]
    for r in range(cells):
        got = pick(spread(post_map[r : r + 1, :], parts[0]), lane_of)
        parts[r % 4] = jnp.where(row_of == r, got, parts[r % 4])
    post2 = 2.0 * ((parts[0] + parts[1]) + (parts[2] + parts[3]))
    for q in range(NA):
        by_chunk(comps_a, q, post2 * links_f[q])
    slot_a[...] = slot_sums(comps_a)
    pack(slot_a, NA, send_a)
    recv_a[own] = send_a[me]

    def send_push(o):
        for z in (e, oe):
            p, target = peer_of(o, z)
            remote(send_a.at[p], recv_a.at[own], fs, fr, target).start()

    loop(1, owners, send_push)
    remote(send_a.at[me], recv_a.at[own], fs, fr, dev(a, b, oe)).start()

    for k in (5, 6, 9, 10):
        small_in[k].wait()
    wait_bytes(zin, zr)
    iz = lax.broadcasted_iota(I32, (span_z, span_y), 0)
    def streamed(x):
        for i in range(19):
            cx, cy, cz = VEL[i]
            sx = x - cx
            inside = 0 <= sx < span_x
            if inside:
                v = relaxed[i, sx * span_z : (sx + 1) * span_z, :]
            else:
                s = 0 if cx > 0 else 1
                v = xin[s, XD[s].index(i)]
            if cz:
                s = 0 if cz > 0 else 1
                if inside:
                    edge = zin[s, ZD[s].index(i), sx : sx + 1, :]
                else:
                    sxx = 0 if cx > 0 else 1
                    j = XZD[sxx].index(i)
                    edge = ein[sxx, j : j + 1, :]
                v = pltpu.roll(v, 1 if cz > 0 else span_z - 1, 0)
                v = jnp.where(iz == (0 if cz > 0 else span_z - 1), edge, v)
            if cy:
                v = pltpu.roll(v, 1 if cy > 0 else span_y - 1, 1)
            nxt[i, x] = v

    for x in range(1, span_x - 1):
        streamed(x)

    state[0:16, :] = jnp.concatenate(
        [bpos[...], bquat[...], bvel[...], bspin[...], iinert[...]], 0
    )
    state[16:17, :] = imass[...]

    wait_bytes(motion_all.at[pl.ds(0, owners - 1)], mr)
    local_b = spread(local_row, lane_t)

    def gather_motion(o, acc):
        return jnp.where(owner_row == o, pick(motion_all[o], local_b), acc)

    slot_motion = lax.fori_loop(0, owners, gather_motion, jnp.zeros(tile, F32), unroll=unroll)
    along = None
    for q in range(6):
        t = links_f[q] * pick(spread(slot_motion[q : q + 1, :], slot), slot)
        along = t if along is None else along + t
    drop = links_f[6] * along
    drop_hi = drop.astype(BF16).astype(F32)
    drops = jnp.concatenate([at_lanes(drop_hi), at_lanes(drop - drop_hi)], 0)
    wall = dot(row_hot[...], drops, 1, 1)
    post_map[...] = post_map[...] - (wall[:, 0:span_y] + wall[:, span_y : 2 * span_y])

    wait_bytes(yin, yr)
    lane_c = lax.broadcasted_iota(I32, (8, cells), 1)
    z_c = lane_c - (lane_c // span_z) * span_z
    sub_c = lax.broadcasted_iota(I32, (8, cells), 0)
    both = []
    for s in range(2):
        t0, t1, t2, t3 = (yin[s, k] for k in range(4))
        out = t0
        for j, d in enumerate(YD[s]):
            cx, _, cz = VEL[d]
            if cx == 1:
                v = jnp.where(lane_c < span_z, pltpu.roll(t1, span_z, 1), pltpu.roll(t0, span_z, 1))
            elif cx == -1:
                v = jnp.where(
                    lane_c >= cells - span_z,
                    pltpu.roll(t2, cells - span_z, 1),
                    pltpu.roll(t0, cells - span_z, 1),
                )
            elif cz == 1:
                v = jnp.where(z_c == 0, pltpu.roll(t3, cells - span_z + 1, 1), pltpu.roll(t0, 1, 1))
            elif cz == -1:
                v = jnp.where(
                    z_c == span_z - 1, pltpu.roll(t3, span_z - 1, 1), pltpu.roll(t0, cells - 1, 1)
                )
            else:
                continue
            out = jnp.where(sub_c == j, v, out)
        both.append(out)
    both.append(jnp.zeros((span_y - 16, cells), F32))
    ycols[...] = jnp.concatenate(both, 0).T

    wait_bytes(xin, xr)
    wait_bytes(ein, er)
    streamed(0)
    streamed(span_x - 1)

    wait_bytes(sendx, hs)
    wait_bytes(sende, hs)
    wait_bytes(yin, hs)
    wait_bytes(sendz, hs)
    wait_bytes(motion_all.at[pl.ds(0, owners - 1)], ms)
    wait_bytes(recv_m.at[pl.ds(0, devices - 1)], rs)
    wait_bytes(recv_a.at[pl.ds(0, devices - 1)], fs)

    wait_bytes(recv_m.at[pl.ds(0, devices - 1)], rr)
    wait_bytes(recv_a.at[pl.ds(0, devices - 1)], fr)
    got_m[...] = recv_m[...]
    got_a[...] = recv_a[...]


def finish(
    cap, nxt, bounce_map, dmap, ycols, state, got_m, got_a, a_out, b_out, done, result, sems
):
    span_x, span_z, span_y = nxt.shape[1:]
    iy = lax.broadcasted_iota(I32, (span_z, span_y), 1)
    out = [pltpu.make_async_copy(nxt.at[0], a_out.at[0], sems.at[1])]
    out[0].start()
    chunk = span_x // OUT_CHUNKS
    for x in range(span_x):
        rows = slice(x * span_z, (x + 1) * span_z)
        at = dmap[rows, :]
        bounce = bounce_map[rows, :]
        for i in range(1, 19):
            cy = VEL[i][1]
            v = nxt[i, x]
            if cy:
                s = 0 if cy > 0 else 1
                j = 8 * s + YD[s].index(i)
                v = jnp.where(iy == (0 if cy > 0 else span_y - 1), ycols[rows, j : j + 1], v)
            done[i - 1, x] = jnp.where(at == OPP[i], bounce, v)
        if x % chunk == chunk - 1:
            part = pl.ds(x + 1 - chunk, chunk)
            c = pltpu.make_async_copy(
                done.at[:, part], a_out.at[pl.ds(1, 18), part], sems.at[2 + x // chunk]
            )
            c.start()
            out.append(c)
    devices, slots = got_a.shape[0], got_a.shape[2]
    per_row = slots // cap
    m_rows = got_m.shape[1] - 1
    groups = NM_PAD // SUB
    sub_t = lax.broadcasted_iota(I32, (SUB, slots), 0)

    def gather(k, acc):
        rank = spread(got_m[k, m_rows : m_rows + 1, :], sub_t).astype(I32) - 1
        known = rank >= 0
        safe = sub_t * cap + jnp.clip(rank, 0, cap - 1)
        added = []
        for g in range(groups):
            r, base = (g * SUB) // per_row, (g * SUB) % per_row
            added.append(pick(spread(got_m[k, r : r + 1, :], safe), safe + base * cap))
        added.append(pick(spread(got_a[k], safe), safe))
        return tuple(v + jnp.where(known, w, 0.0) for v, w in zip(acc, added))

    zero = jnp.zeros((SUB, slots), F32)
    sums = lax.fori_loop(0, devices, gather, (zero,) * (groups + 1), unroll=devices <= 32)
    f = [sums[groups][i : i + 1, :] for i in range(6)]
    u = [state[7 + i : 8 + i, :] for i in range(6)]
    for q, (i, j) in enumerate(PAIRS):
        m = sums[q // SUB][q % SUB : q % SUB + 1, :]
        f[i] = f[i] - m * u[j]
        if i != j:
            f[j] = f[j] - m * u[i]
    pos = [state[i : i + 1, :] for i in range(3)]
    qw, qx, qy, qz = (state[3 + i : 4 + i, :] for i in range(4))
    vel, turn = u[0:3], u[3:6]
    inert = [state[13 + i : 14 + i, :] for i in range(3)]
    imass = state[16:17, :]
    velo = [vel[i] + imass * f[i] for i in range(3)]
    velo[2] = velo[2] - GRAV
    rot = [
        [1.0 - 2.0 * (qy * qy + qz * qz), 2.0 * (qx * qy - qw * qz), 2.0 * (qx * qz + qw * qy)],
        [2.0 * (qx * qy + qw * qz), 1.0 - 2.0 * (qx * qx + qz * qz), 2.0 * (qy * qz - qw * qx)],
        [2.0 * (qx * qz - qw * qy), 2.0 * (qy * qz + qw * qx), 1.0 - 2.0 * (qx * qx + qy * qy)],
    ]
    tq = f[3:6]
    acc = [
        inert[c] * (rot[0][c] * tq[0] + rot[1][c] * tq[1] + rot[2][c] * tq[2]) for c in range(3)
    ]
    spin = [
        turn[r] + (rot[r][0] * acc[0] + rot[r][1] * acc[1] + rot[r][2] * acc[2]) for r in range(3)
    ]
    sx, sy, sz = spin
    dq = [
        -(sx * qx + sy * qy + sz * qz),
        sx * qw + sy * qz - sz * qy,
        sy * qw + sz * qx - sx * qz,
        sz * qw + sx * qy - sy * qx,
    ]
    scale = lax.rsqrt(1.0 + 0.25 * (sx * sx + sy * sy + sz * sz))
    quat = [(q + 0.5 * k) * scale for q, k in zip((qw, qx, qy, qz), dq)]
    rows = [pos[i] + velo[i] for i in range(3)] + quat + velo + spin
    for i, v in enumerate(rows):
        result[i : i + 1, :] = v
    small = pltpu.make_async_copy(result, b_out, sems.at[0])
    small.start()
    for c in out:
        c.wait()
    small.wait()


def shards(sizes, *args):
    pop = args[0]
    span_x, span_z, span_y = pop.shape[1:]
    cells = span_x * span_z
    body_own = args[6].shape[1]
    slots = args[5].shape[-1]
    links = args[1].shape[-1]
    chunks = links // span_y
    owners = sizes[0] * sizes[1]
    devices = 2 * owners
    cap = max(1, 2 * slots // owners)
    m_rows = -(-NM // (slots // cap))
    args = list(args)
    for k in (1, 2, 3):
        args[k] = args[k].reshape(chunks, span_y)
    args[4] = args[4].reshape(3 * chunks, span_y)
    args[5] = args[5].reshape(1, slots)
    args[10] = args[10].reshape(1, -1)
    vm = pl.BlockSpec(memory_space=pltpu.VMEM)
    dma = pltpu.SemaphoreType.DMA
    V = lambda *s: pltpu.VMEM(s, F32)
    args = [pltpu.with_memory_space_constraint(v, pltpu.MemorySpace.HBM) for v in args]
    hbm = pl.BlockSpec(memory_space=pltpu.MemorySpace.HBM)
    outs = pl.pallas_call(
        functools.partial(kernel, (sizes[0], sizes[1], cap)),
        out_shape=(
            jax.ShapeDtypeStruct(pop.shape, F32),
            jax.ShapeDtypeStruct((cells, span_y), F32),
            jax.ShapeDtypeStruct((cells, span_y), I32),
            jax.ShapeDtypeStruct((cells, span_y), F32),
            jax.ShapeDtypeStruct((24, body_own), F32),
            jax.ShapeDtypeStruct((devices, m_rows + 1, slots), F32),
            jax.ShapeDtypeStruct((devices, 1, slots), F32),
        ),
        in_specs=[hbm] * len(args),
        out_specs=(vm,) * 7,
        scratch_shapes=[
            *[pltpu.VMEM(v.shape, v.dtype) for v in args],
            V(19, cells, span_y),
            V(2, 5, span_z, span_y), V(2, 5, span_z, span_y),
            V(2, 5, span_x, span_y), V(2, 5, span_x, span_y),
            V(2, 8, span_y), V(2, 8, span_y),
            V(2, 8, cells), V(2, 4, 8, cells),
            V(7, SUB, span_y), V(chunks, NM_PAD, span_y), V(chunks, SUB, span_y),
            pltpu.VMEM((owners * cap, links), BF16), pltpu.VMEM((cells, links), BF16),
            V(NM_PAD, owners * cap), V(SUB, owners * cap),
            V(8, body_own), V(owners, 8, body_own),
            V(owners, m_rows + 1, slots), V(devices, m_rows + 1, slots),
            V(owners, 1, slots), V(devices, 1, slots),
            *[dma] * 11,
            dma((POP_CHUNKS,)), dma((11,)),
        ],
        compiler_params=pltpu.CompilerParams(
            collective_id=0, has_side_effects=True, vmem_limit_bytes=K1_VMEM
        ),
        name="lattice_step",
    )(*args)
    return pl.pallas_call(
        functools.partial(finish, cap),
        out_shape=(
            jax.ShapeDtypeStruct(pop.shape, F32),
            jax.ShapeDtypeStruct((13, body_own), F32),
        ),
        in_specs=[vm] * 7,
        out_specs=(hbm, hbm),
        scratch_shapes=[V(18, *pop.shape[1:]), V(13, body_own), dma((2 + OUT_CHUNKS,))],
        compiler_params=pltpu.CompilerParams(vmem_limit_bytes=K2_VMEM),
        name="finish",
    )(*outs)


def solution(mesh):
    sizes = (mesh.shape["gx"], mesh.shape["gy"])
    link = P("gx", "gz", "gy", None)
    body = P(None, ("gx", "gy"))
    return jax.shard_map(
        functools.partial(shards, sizes),
        mesh=mesh,
        in_specs=(
            P(None, "gx", "gz", "gy"), link, link, link, P(None, "gx", "gz", "gy", None), link,
            body, body, body, body, P(("gx", "gy")), body,
        ),
        out_specs=(P(None, "gx", "gz", "gy"), body),
        check_vma=False,
    )
```

```python
import functools

import jax
import jax.numpy as jnp
import numpy as np
from jax import lax
from jax.experimental import pallas as pl
from jax.experimental.pallas import tpu as pltpu
from jax.sharding import PartitionSpec as P

VEL = [
    (0, 0, 0), (1, 0, 0), (-1, 0, 0), (0, 1, 0), (0, -1, 0), (0, 0, 1), (0, 0, -1),
    (1, 1, 0), (-1, -1, 0), (1, -1, 0), (-1, 1, 0), (1, 0, 1), (-1, 0, -1), (1, 0, -1),
    (-1, 0, 1), (0, 1, 1), (0, -1, -1), (0, 1, -1), (0, -1, 1),
]
WT = [1.0 / 3.0] + [1.0 / 18.0] * 6 + [1.0 / 36.0] * 12
OPP = [0, 2, 1, 4, 3, 6, 5, 8, 7, 10, 9, 12, 11, 14, 13, 16, 15, 18, 17]
OMEGA = 1.25
POP_CHUNKS = 4
OUT_CHUNKS = 4
K1_VMEM = 24 * 1024 * 1024
K2_VMEM = 4 * 1024 * 1024
GRAV = 0.02
F32 = jnp.float32
BF16 = jnp.bfloat16
I32 = jnp.int32
SUB = 8
PAIRS = [(i, j) for i in range(6) for j in range(i, 6)]
NA = 6
NM = len(PAIRS)
NM_PAD = 24


def dirs_of(comp, sign):
    return [d for d in range(19) if VEL[d][comp] == sign]


XD = (dirs_of(0, 1), dirs_of(0, -1))
YD = (dirs_of(1, 1), dirs_of(1, -1))
ZD = (dirs_of(2, 1), dirs_of(2, -1))
XZD = tuple([d for d in XD[s] if VEL[d][2] != 0] for s in range(2))


def dot(a, b, ca, cb):
    return lax.dot_general(a, b, (((ca,), (cb,)), ((), ())), preferred_element_type=F32)


def stacked(v):
    hi = v.astype(BF16).astype(F32)
    return jnp.concatenate([hi, v - hi], 0).astype(BF16)


def unstacked(v):
    k = v.shape[0] // 2
    return v[0:k] + v[k : 2 * k]


def pick(table, index):
    index = jnp.clip(index, 0, table.shape[1] - 1)
    return jnp.take_along_axis(table, index, axis=1, mode="promise_in_bounds")


def spread(row, like):
    return jnp.broadcast_to(row, like.shape)


def kernel(
    sizes,
    pop_h, *rest,
):
    small_h, outs, rest = rest[:11], rest[11:18], rest[18:]
    pop, small, rest = rest[0], rest[1:12], rest[12:]
    step(sizes, pop_h, small_h, pop, *small, *outs, *rest)


def step(
    sizes, pop_h, small_h,
    pop, lcell, ldir, lslot, larm, bb_ref, bpos, bquat, bvel, bspin, imass, iinert,
    nxt, post_map, dmap, ycols, state, got_m, got_a,
    relaxed, sendx, xin, sendz, zin, sende, ein, sendy, yin,
    links_f, comps_m, comps_a, place_hot, row_hot, slot_m, slot_a,
    motion_own, motion_all, send_m, recv_m, send_a, recv_a,
    hs, xr, er, yr, zr, ms, mr, rs, rr, fs, fr, ps, ss,
):
    ngx, ngy, cap = sizes
    owners = ngx * ngy
    devices = 2 * owners
    span_x, span_z, span_y = pop.shape[1:]
    cells = span_x * span_z
    body_own = bvel.shape[1]
    slots = bb_ref.shape[-1]
    chunks = lcell.shape[0]
    per_row = slots // cap
    m_rows = recv_m.shape[1] - 1
    a, b, e = lax.axis_index("gx"), lax.axis_index("gy"), lax.axis_index("gz")
    me = a * ngy + b
    own = me * 2 + e
    ap, am = lax.rem(a + 1, ngx), lax.rem(a + ngx - 1, ngx)
    bp, bm = lax.rem(b + 1, ngy), lax.rem(b + ngy - 1, ngy)
    oe = 1 - e

    def dev(x, y, z):
        return {"gx": x, "gy": y, "gz": z}

    def peer_of(offset, z):
        p = lax.rem(me + offset, owners)
        return p, dev(p // ngy, lax.rem(p, ngy), z)

    unroll = owners <= 16

    def loop(lo, hi, body):
        if unroll:
            for i in range(lo, hi):
                body(i)
        else:
            pl.loop(lo, hi)(body)

    def remote(src, dst, send_sem, recv_sem, target):
        return pltpu.make_async_remote_copy(
            src_ref=src, dst_ref=dst, send_sem=send_sem, recv_sem=recv_sem,
            device_id=target, device_id_type=pl.DeviceIdType.MESH,
        )

    def wait_bytes(ref, sem):
        pltpu.make_async_copy(ref, ref, sem).wait()

    small = (lcell, ldir, lslot, larm, bb_ref, bpos, bquat, bvel, bspin, imass, iinert)
    small_in = [
        pltpu.make_async_copy(src, dst, ss.at[k]) for k, (src, dst) in enumerate(zip(small_h, small))
    ]
    chunk = span_x // POP_CHUNKS
    pop_in = [
        pltpu.make_async_copy(
            pop_h.at[:, pl.ds(k * chunk, chunk)], pop.at[:, pl.ds(k * chunk, chunk)], ps.at[k]
        )
        for k in range(POP_CHUNKS)
    ]
    for k in (4, 0, 1, 2, 3):
        small_in[k].start()
    for c in pop_in:
        c.start()
    for k in (7, 8, 5, 6, 9, 10):
        small_in[k].start()

    barrier = pltpu.get_barrier_semaphore()

    def greet(o):
        for z in (e, oe):
            pl.semaphore_signal(
                barrier, inc=1, device_id=peer_of(o, z)[1], device_id_type=pl.DeviceIdType.MESH
            )

    loop(1, owners, greet)
    pl.semaphore_signal(
        barrier, inc=1, device_id=dev(a, b, oe), device_id_type=pl.DeviceIdType.MESH
    )

    tile = (SUB, span_y)
    lane_t = lax.broadcasted_iota(I32, tile, 1)
    sub_t = lax.broadcasted_iota(I32, tile, 0)

    small_in[4].wait()
    bodies = bb_ref[...]
    owner_row = bodies // body_own
    local_row = bodies - owner_row * body_own
    sq = (slots, slots)
    owner_b = jnp.broadcast_to(owner_row.astype(F32), sq)
    iota_0 = lax.broadcasted_iota(I32, sq, 0)
    iota_1 = lax.broadcasted_iota(I32, sq, 1)
    earlier = jnp.where((owner_b == owner_b.T) & (iota_0 < iota_1), 1.0, 0.0)
    rank_row = jnp.sum(earlier, axis=0, keepdims=True)
    iota_o = lax.broadcasted_iota(I32, (owners, slots), 0)
    owned = iota_o == owner_row
    by_owner = jnp.where(owned, rank_row + 1.0, 0.0).astype(BF16)
    place = jnp.where(iota_0 == local_row, 1.0, 0.0).astype(BF16)
    rank_of = dot(by_owner, place, 1, 1)
    place_row = owner_row * cap + rank_row.astype(I32)
    for o in range(owners):
        send_m[o, m_rows : m_rows + 1, :] = rank_of[o : o + 1, :]
    lane_block = lane_t // cap
    unpack = sub_t * cap + lane_t - lane_block * cap

    def pack(src, count, dst):
        for g in range(owners // SUB):
            first = g * SUB * cap
            half = slice(first // slots * slots, first // slots * slots + slots)
            index = unpack + first % slots
            for r in range(-(-count // per_row)):
                out = jnp.zeros(tile, F32)
                for k in range(min(per_row, count - r * per_row)):
                    c = r * per_row + k
                    got = pick(spread(src[c : c + 1, half], out), index)
                    out = jnp.where(lane_block == k, got, out)
                for s in range(SUB):
                    dst[g * SUB + s, r : r + 1, :] = out[s : s + 1, :]

    for k in (0, 1, 2, 3):
        small_in[k].wait()
    cell = lcell[...]
    dirs = ldir[...]
    slot = lslot[...]
    row_of = cell // span_y
    lane_of = cell - row_of * span_y
    vel = []
    for c in range(3):
        v = jnp.zeros(tile, F32)
        for d in range(1, 19):
            if VEL[d][c]:
                v = jnp.where(dirs == d, float(VEL[d][c]), v)
        vel.append(v)
    six_w = jnp.where(dirs > 6, 6.0 * WT[7], 6.0 * WT[1])
    arm = [larm[SUB * i : SUB * (i + 1), :] for i in range(3)]
    f6 = vel + [
        arm[1] * vel[2] - arm[2] * vel[1],
        arm[2] * vel[0] - arm[0] * vel[2],
        arm[0] * vel[1] - arm[1] * vel[0],
    ]
    for q in range(6):
        links_f[q] = f6[q]
    links_f[6] = six_w
    wf = [six_w * v for v in f6]

    def by_chunk(comps, q, value):
        for j in range(chunks):
            comps[j, q : q + 1, :] = value[j : j + 1, :]

    for q, (i, j) in enumerate(PAIRS):
        by_chunk(comps_m, q, wf[i] * f6[j])
    for j in range(chunks):
        comps_m[j, NM:NM_PAD, :] = jnp.zeros((NM_PAD - NM, span_y), F32)
        comps_a[j, NA:SUB, :] = jnp.zeros((SUB - NA, span_y), F32)
    link_place = pick(spread(place_row, slot), slot)
    iota_p = lax.broadcasted_iota(I32, (owners * cap, span_y), 0)
    for j in range(chunks):
        place_hot[:, j * span_y : (j + 1) * span_y] = jnp.where(
            iota_p == link_place[j : j + 1, :], 1.0, 0.0
        ).astype(BF16)

    def slot_sums(comps):
        v = jnp.concatenate([comps[j] for j in range(chunks)], 1)
        return unstacked(dot(stacked(v), place_hot[...], 1, 1))

    slot_m[...] = slot_sums(comps_m)
    pack(slot_m, NM, send_m)

    iota_c = lax.broadcasted_iota(I32, (cells, span_y), 0)
    iota_y = lax.broadcasted_iota(I32, (span_y, span_y), 0)

    def at_lanes(value):
        return jnp.concatenate(
            [
                jnp.where(iota_y == lane_of[j : j + 1, :], value[j : j + 1, :], 0.0).astype(BF16)
                for j in range(chunks)
            ],
            1,
        )

    for j in range(chunks):
        row_hot[:, j * span_y : (j + 1) * span_y] = jnp.where(
            iota_c == row_of[j : j + 1, :], 1.0, 0.0
        ).astype(BF16)
    dmap[...] = dot(row_hot[...], at_lanes(dirs.astype(F32)), 1, 1).astype(I32)

    for x in range(span_x):
        if x % chunk == 0:
            pop_in[x // chunk].wait()
        for z in range(0, span_z, SUB):
            f = [pop[d, x, z : z + SUB, :] for d in range(19)]
            rho = f[0]
            for d in range(1, 19):
                rho = rho + f[d]
            inv = 1.0 / rho
            u = []
            for c in range(3):
                pos, neg = dirs_of(c, 1), dirs_of(c, -1)
                tot = f[pos[0]] - f[neg[0]]
                for p, q in zip(pos[1:], neg[1:]):
                    tot = tot + (f[p] - f[q])
                u.append(tot * inv)
            usq = 1.0 - 1.5 * (u[0] * u[0] + u[1] * u[1] + u[2] * u[2])
            rows = pl.ds(x * span_z + z, SUB)
            keep = 1.0 - OMEGA
            relaxed[0, rows, :] = keep * f[0] + (OMEGA * WT[0]) * rho * usq
            at = dmap[rows, :]
            post = jnp.zeros(tile, F32)
            for d in range(1, 19, 2):
                terms = [u[c] if VEL[d][c] > 0 else -u[c] for c in range(3) if VEL[d][c]]
                proj = terms[0] if len(terms) == 1 else terms[0] + terms[1]
                scale = (OMEGA * WT[d]) * rho
                even = scale * (usq + 4.5 * proj * proj)
                odd = scale * (3.0 * proj)
                v = keep * f[d] + (even + odd)
                relaxed[d, rows, :] = v
                post = jnp.where(at == d, v, post)
                v = keep * f[d + 1] + (even - odd)
                relaxed[d + 1, rows, :] = v
                post = jnp.where(at == d + 1, v, post)
            post_map[rows, :] = post

    lane = lax.broadcasted_iota(I32, (cells, span_y), 1)
    packed = jnp.zeros((cells, span_y), F32)
    for s in range(2):
        ye = (span_y - 1) if s == 0 else 0
        for j, d in enumerate(YD[s]):
            packed = jnp.where(lane == 8 * s + j, relaxed[d, :, ye : ye + 1], packed)
    pack_t = packed.T
    for s in range(2):
        sendy[s] = pack_t[8 * s : 8 * s + 8, :]
    for s in range(2):
        xe = (span_x - 1) if s == 0 else 0
        ze = (span_z - 1) if s == 0 else 0
        for j, d in enumerate(XD[s]):
            sendx[s, j] = relaxed[d, xe * span_z : (xe + 1) * span_z, :]
        for j, d in enumerate(ZD[s]):
            for x in range(span_x):
                r = x * span_z + ze
                sendz[s, j, x : x + 1, :] = relaxed[d, r : r + 1, :]
        sende[s] = jnp.zeros(sende.shape[1:], F32)
        for j, d in enumerate(XZD[s]):
            r = xe * span_z + ((span_z - 1) if VEL[d][2] > 0 else 0)
            sende[s, j : j + 1, :] = relaxed[d, r : r + 1, :]

    small_in[7].wait()
    small_in[8].wait()
    motion_own[...] = jnp.concatenate(
        [bvel[...], bspin[...], jnp.zeros((2, body_own), F32)], 0
    )
    motion_all[me] = motion_own[...]
    recv_m[own] = send_m[me]

    pl.semaphore_wait(barrier, devices - 1)

    remote(sendz, zin, hs, zr, dev(a, b, oe)).start()
    for s in range(2):
        xt, yt = (ap, bp) if s == 0 else (am, bm)
        for k, t in enumerate((dev(a, yt, e), dev(ap, yt, e), dev(am, yt, e), dev(a, yt, oe))):
            remote(sendy.at[s], yin.at[s, k], hs, yr, t).start()

    def send_motion(o):
        remote(motion_own, motion_all.at[me], ms, mr, peer_of(o, e)[1]).start()

    loop(1, owners, send_motion)

    for s in range(2):
        xt, yt = (ap, bp) if s == 0 else (am, bm)
        remote(sendx.at[s], xin.at[s], hs, xr, dev(xt, b, e)).start()
        remote(sende.at[s], ein.at[s], hs, er, dev(xt, b, oe)).start()

    parts = [jnp.zeros(tile, F32) for _ in range(4)]
    for r in range(cells):
        got = pick(spread(post_map[r : r + 1, :], parts[0]), lane_of)
        parts[r % 4] = jnp.where(row_of == r, got, parts[r % 4])
    post2 = 2.0 * ((parts[0] + parts[1]) + (parts[2] + parts[3]))
    for q in range(NA):
        by_chunk(comps_a, q, post2 * links_f[q])
    slot_a[...] = slot_sums(comps_a)
    pack(slot_a, NA, send_a)
    recv_a[own] = send_a[me]

    def send_push(o):
        for z in (e, oe):
            p, target = peer_of(o, z)
            remote(send_a.at[p], recv_a.at[own], fs, fr, target).start()

    loop(1, owners, send_push)
    remote(send_a.at[me], recv_a.at[own], fs, fr, dev(a, b, oe)).start()

    def send_response(o):
        for z in (e, oe):
            p, target = peer_of(o, z)
            remote(send_m.at[p], recv_m.at[own], rs, rr, target).start()

    loop(1, owners, send_response)
    remote(send_m.at[me], recv_m.at[own], rs, rr, dev(a, b, oe)).start()

    for k in (5, 6, 9, 10):
        small_in[k].wait()
    wait_bytes(zin, zr)
    iz = lax.broadcasted_iota(I32, (span_z, span_y), 0)
    def streamed(x):
        for i in range(19):
            cx, cy, cz = VEL[i]
            sx = x - cx
            inside = 0 <= sx < span_x
            if inside:
                v = relaxed[i, sx * span_z : (sx + 1) * span_z, :]
            else:
                s = 0 if cx > 0 else 1
                v = xin[s, XD[s].index(i)]
            if cz:
                s = 0 if cz > 0 else 1
                if inside:
                    edge = zin[s, ZD[s].index(i), sx : sx + 1, :]
                else:
                    sxx = 0 if cx > 0 else 1
                    j = XZD[sxx].index(i)
                    edge = ein[sxx, j : j + 1, :]
                v = pltpu.roll(v, 1 if cz > 0 else span_z - 1, 0)
                v = jnp.where(iz == (0 if cz > 0 else span_z - 1), edge, v)
            if cy:
                v = pltpu.roll(v, 1 if cy > 0 else span_y - 1, 1)
            nxt[i, x] = v

    for x in range(1, span_x - 1):
        streamed(x)

    state[0:16, :] = jnp.concatenate(
        [bpos[...], bquat[...], bvel[...], bspin[...], iinert[...]], 0
    )
    state[16:17, :] = imass[...]

    wait_bytes(motion_all.at[pl.ds(0, owners - 1)], mr)
    local_b = spread(local_row, lane_t)

    def gather_motion(o, acc):
        return jnp.where(owner_row == o, pick(motion_all[o], local_b), acc)

    slot_motion = lax.fori_loop(0, owners, gather_motion, jnp.zeros(tile, F32), unroll=unroll)
    along = None
    for q in range(6):
        t = links_f[q] * pick(spread(slot_motion[q : q + 1, :], slot), slot)
        along = t if along is None else along + t
    drop = links_f[6] * along
    drop_hi = drop.astype(BF16).astype(F32)
    drops = jnp.concatenate([at_lanes(drop_hi), at_lanes(drop - drop_hi)], 0)
    wall = dot(row_hot[...], drops, 1, 1)
    post_map[...] = post_map[...] - (wall[:, 0:span_y] + wall[:, span_y : 2 * span_y])

    wait_bytes(yin, yr)
    lane_c = lax.broadcasted_iota(I32, (8, cells), 1)
    z_c = lane_c - (lane_c // span_z) * span_z
    sub_c = lax.broadcasted_iota(I32, (8, cells), 0)
    both = []
    for s in range(2):
        t0, t1, t2, t3 = (yin[s, k] for k in range(4))
        out = t0
        for j, d in enumerate(YD[s]):
            cx, _, cz = VEL[d]
            if cx == 1:
                v = jnp.where(lane_c < span_z, pltpu.roll(t1, span_z, 1), pltpu.roll(t0, span_z, 1))
            elif cx == -1:
                v = jnp.where(
                    lane_c >= cells - span_z,
                    pltpu.roll(t2, cells - span_z, 1),
                    pltpu.roll(t0, cells - span_z, 1),
                )
            elif cz == 1:
                v = jnp.where(z_c == 0, pltpu.roll(t3, cells - span_z + 1, 1), pltpu.roll(t0, 1, 1))
            elif cz == -1:
                v = jnp.where(
                    z_c == span_z - 1, pltpu.roll(t3, span_z - 1, 1), pltpu.roll(t0, cells - 1, 1)
                )
            else:
                continue
            out = jnp.where(sub_c == j, v, out)
        both.append(out)
    both.append(jnp.zeros((span_y - 16, cells), F32))
    ycols[...] = jnp.concatenate(both, 0).T

    wait_bytes(xin, xr)
    wait_bytes(ein, er)
    streamed(0)
    streamed(span_x - 1)

    wait_bytes(sendx, hs)
    wait_bytes(sende, hs)
    wait_bytes(yin, hs)
    wait_bytes(sendz, hs)
    wait_bytes(motion_all.at[pl.ds(0, owners - 1)], ms)
    wait_bytes(recv_m.at[pl.ds(0, devices - 1)], rs)
    wait_bytes(recv_a.at[pl.ds(0, devices - 1)], fs)

    wait_bytes(recv_m.at[pl.ds(0, devices - 1)], rr)
    wait_bytes(recv_a.at[pl.ds(0, devices - 1)], fr)
    got_m[...] = recv_m[...]
    got_a[...] = recv_a[...]


def finish(
    cap, nxt, bounce_map, dmap, ycols, state, got_m, got_a, a_out, b_out, done, result, sems
):
    span_x, span_z, span_y = nxt.shape[1:]
    iy = lax.broadcasted_iota(I32, (span_z, span_y), 1)
    out = [pltpu.make_async_copy(nxt.at[0], a_out.at[0], sems.at[1])]
    out[0].start()
    chunk = span_x // OUT_CHUNKS
    for x in range(span_x):
        rows = slice(x * span_z, (x + 1) * span_z)
        at = dmap[rows, :]
        bounce = bounce_map[rows, :]
        for i in range(1, 19):
            cy = VEL[i][1]
            v = nxt[i, x]
            if cy:
                s = 0 if cy > 0 else 1
                j = 8 * s + YD[s].index(i)
                v = jnp.where(iy == (0 if cy > 0 else span_y - 1), ycols[rows, j : j + 1], v)
            done[i - 1, x] = jnp.where(at == OPP[i], bounce, v)
        if x % chunk == chunk - 1:
            part = pl.ds(x + 1 - chunk, chunk)
            c = pltpu.make_async_copy(
                done.at[:, part], a_out.at[pl.ds(1, 18), part], sems.at[2 + x // chunk]
            )
            c.start()
            out.append(c)
    devices, slots = got_a.shape[0], got_a.shape[2]
    per_row = slots // cap
    m_rows = got_m.shape[1] - 1
    groups = NM_PAD // SUB
    sub_t = lax.broadcasted_iota(I32, (SUB, slots), 0)

    def gather(k, acc):
        rank = spread(got_m[k, m_rows : m_rows + 1, :], sub_t).astype(I32) - 1
        known = rank >= 0
        safe = sub_t * cap + jnp.clip(rank, 0, cap - 1)
        added = []
        for g in range(groups):
            r, base = (g * SUB) // per_row, (g * SUB) % per_row
            added.append(pick(spread(got_m[k, r : r + 1, :], safe), safe + base * cap))
        added.append(pick(spread(got_a[k], safe), safe))
        return tuple(v + jnp.where(known, w, 0.0) for v, w in zip(acc, added))

    zero = jnp.zeros((SUB, slots), F32)
    sums = lax.fori_loop(0, devices, gather, (zero,) * (groups + 1), unroll=devices <= 32)
    f = [sums[groups][i : i + 1, :] for i in range(6)]
    u = [state[7 + i : 8 + i, :] for i in range(6)]
    for q, (i, j) in enumerate(PAIRS):
        m = sums[q // SUB][q % SUB : q % SUB + 1, :]
        f[i] = f[i] - m * u[j]
        if i != j:
            f[j] = f[j] - m * u[i]
    pos = [state[i : i + 1, :] for i in range(3)]
    qw, qx, qy, qz = (state[3 + i : 4 + i, :] for i in range(4))
    vel, turn = u[0:3], u[3:6]
    inert = [state[13 + i : 14 + i, :] for i in range(3)]
    imass = state[16:17, :]
    velo = [vel[i] + imass * f[i] for i in range(3)]
    velo[2] = velo[2] - GRAV
    rot = [
        [1.0 - 2.0 * (qy * qy + qz * qz), 2.0 * (qx * qy - qw * qz), 2.0 * (qx * qz + qw * qy)],
        [2.0 * (qx * qy + qw * qz), 1.0 - 2.0 * (qx * qx + qz * qz), 2.0 * (qy * qz - qw * qx)],
        [2.0 * (qx * qz - qw * qy), 2.0 * (qy * qz + qw * qx), 1.0 - 2.0 * (qx * qx + qy * qy)],
    ]
    tq = f[3:6]
    acc = [
        inert[c] * (rot[0][c] * tq[0] + rot[1][c] * tq[1] + rot[2][c] * tq[2]) for c in range(3)
    ]
    spin = [
        turn[r] + (rot[r][0] * acc[0] + rot[r][1] * acc[1] + rot[r][2] * acc[2]) for r in range(3)
    ]
    sx, sy, sz = spin
    dq = [
        -(sx * qx + sy * qy + sz * qz),
        sx * qw + sy * qz - sz * qy,
        sy * qw + sz * qx - sx * qz,
        sz * qw + sx * qy - sy * qx,
    ]
    scale = lax.rsqrt(1.0 + 0.25 * (sx * sx + sy * sy + sz * sz))
    quat = [(q + 0.5 * k) * scale for q, k in zip((qw, qx, qy, qz), dq)]
    rows = [pos[i] + velo[i] for i in range(3)] + quat + velo + spin
    for i, v in enumerate(rows):
        result[i : i + 1, :] = v
    small = pltpu.make_async_copy(result, b_out, sems.at[0])
    small.start()
    for c in out:
        c.wait()
    small.wait()


def shards(sizes, *args):
    pop = args[0]
    span_x, span_z, span_y = pop.shape[1:]
    cells = span_x * span_z
    body_own = args[6].shape[1]
    slots = args[5].shape[-1]
    links = args[1].shape[-1]
    chunks = links // span_y
    owners = sizes[0] * sizes[1]
    devices = 2 * owners
    cap = max(1, 2 * slots // owners)
    m_rows = -(-NM // (slots // cap))
    args = list(args)
    for k in (1, 2, 3):
        args[k] = args[k].reshape(chunks, span_y)
    args[4] = args[4].reshape(3 * chunks, span_y)
    args[5] = args[5].reshape(1, slots)
    args[10] = args[10].reshape(1, -1)
    vm = pl.BlockSpec(memory_space=pltpu.VMEM)
    dma = pltpu.SemaphoreType.DMA
    V = lambda *s: pltpu.VMEM(s, F32)
    args = [pltpu.with_memory_space_constraint(v, pltpu.MemorySpace.HBM) for v in args]
    hbm = pl.BlockSpec(memory_space=pltpu.MemorySpace.HBM)
    outs = pl.pallas_call(
        functools.partial(kernel, (sizes[0], sizes[1], cap)),
        out_shape=(
            jax.ShapeDtypeStruct(pop.shape, F32),
            jax.ShapeDtypeStruct((cells, span_y), F32),
            jax.ShapeDtypeStruct((cells, span_y), I32),
            jax.ShapeDtypeStruct((cells, span_y), F32),
            jax.ShapeDtypeStruct((24, body_own), F32),
            jax.ShapeDtypeStruct((devices, m_rows + 1, slots), F32),
            jax.ShapeDtypeStruct((devices, 1, slots), F32),
        ),
        in_specs=[hbm] * len(args),
        out_specs=(vm,) * 7,
        scratch_shapes=[
            *[pltpu.VMEM(v.shape, v.dtype) for v in args],
            V(19, cells, span_y),
            V(2, 5, span_z, span_y), V(2, 5, span_z, span_y),
            V(2, 5, span_x, span_y), V(2, 5, span_x, span_y),
            V(2, 8, span_y), V(2, 8, span_y),
            V(2, 8, cells), V(2, 4, 8, cells),
            V(7, SUB, span_y), V(chunks, NM_PAD, span_y), V(chunks, SUB, span_y),
            pltpu.VMEM((owners * cap, links), BF16), pltpu.VMEM((cells, links), BF16),
            V(NM_PAD, owners * cap), V(SUB, owners * cap),
            V(8, body_own), V(owners, 8, body_own),
            V(owners, m_rows + 1, slots), V(devices, m_rows + 1, slots),
            V(owners, 1, slots), V(devices, 1, slots),
            *[dma] * 11,
            dma((POP_CHUNKS,)), dma((11,)),
        ],
        compiler_params=pltpu.CompilerParams(
            collective_id=0, has_side_effects=True, vmem_limit_bytes=K1_VMEM
        ),
        name="lattice_step",
    )(*args)
    return pl.pallas_call(
        functools.partial(finish, cap),
        out_shape=(
            jax.ShapeDtypeStruct(pop.shape, F32),
            jax.ShapeDtypeStruct((13, body_own), F32),
        ),
        in_specs=[vm] * 7,
        out_specs=(hbm, hbm),
        scratch_shapes=[V(18, *pop.shape[1:]), V(13, body_own), dma((2 + OUT_CHUNKS,))],
        compiler_params=pltpu.CompilerParams(vmem_limit_bytes=K2_VMEM),
        name="finish",
    )(*outs)


def solution(mesh):
    sizes = (mesh.shape["gx"], mesh.shape["gy"])
    link = P("gx", "gz", "gy", None)
    body = P(None, ("gx", "gy"))
    return jax.shard_map(
        functools.partial(shards, sizes),
        mesh=mesh,
        in_specs=(
            P(None, "gx", "gz", "gy"), link, link, link, P(None, "gx", "gz", "gy", None), link,
            body, body, body, body, P(("gx", "gy")), body,
        ),
        out_specs=(P(None, "gx", "gz", "gy"), body),
        check_vma=False,
    )
```
